256 devices in a mesh: seq: 64 (over y, z, x_hi), tp: 4 (over x_lo, core).
Axes of the slice: x: 4 (x_hi: 2, x_lo: 2; x = x_hi * 2 + x_lo), y: 4, z: 8, core: 2. Of those that a mesh axis runs over, the one named last changes fastest.
Arguments:
- query_input: bfloat16 [8192, 4096], P('seq', 'tp'), may hold values from -6 to 6
- key_input: bfloat16 [8192, 4096], P('seq', 'tp'), may hold values from -6 to 6
- value_input: bfloat16 [8192, 4096], P('seq', 'tp'), may hold values from -6 to 6
- short_filter: float32 [3, 3, 4096], P(None, None, 'tp'), may hold values from -3 to 3
- residues: float32 [16, 4096], P(None, 'tp'), may hold values from -1.5 to 1.5
- decays: float32 [16, 4096], P(None, 'tp'), as said below
- skip_gain: float32 [4096], P('tp'), may hold values from -4 to 4
- head_weight: bfloat16 [32, 4096, 128], P(None, ('tp', 'seq')), may hold values from -0.015625 to 0.015625
Outputs:
- operator_out: bfloat16 [8192, 4096], P('seq', 'tp')
- probe_out: bfloat16 [512, 128], P(('seq', 'tp'))
The draws below stay inside these ranges and needn't reach their ends.
Inputs may be any that keep to these rules, and one draw needn't show every extreme that they name: `decays`: each rate is positive, at least 1 / 16384 and at most 1 / 30.
All inputs are finite; a program needn't handle non-finite values.
Results may differ from the reference program's by a relative error of at most 0.01.
Values may be sent and summed in bfloat16 or wider, within the bound.
No kernel may reach another device: no remote copies, remote signals or barrier semaphores. Data moves between devices by JAX's collectives and lax.ppermute only.
A program may use at most 64 MiB of HBM per device.

```python
import jax
import jax.numpy as jnp
from jax import lax

C = 4096
OUT = 128
ORDER = 16
KERNEL = 32
STRIDE = 16
SEQ_LEN = 8192


def draw_decays(key, part):
    low_rate = 0.5 / SEQ_LEN
    high_rate = 1.0 / 30.0
    key_one = jax.random.fold_in(key, 0)
    unit_draw = jax.random.uniform(key_one, (ORDER, C), jnp.float32)
    wide_rates = jnp.exp(jnp.log(low_rate) + unit_draw * (jnp.log(high_rate) - jnp.log(low_rate)))
    return wide_rates.astype(jnp.float32)


def level_of(rng, shape, shards, low, high):
    def one(position, shards_of):
        draws = jax.random.uniform(jax.random.fold_in(jax.random.fold_in(rng, 6), position), (shards_of,), jnp.float32, low / len(shards), high / len(shards))
        return jnp.repeat(jnp.exp(draws), shape[position] // shards_of).reshape((-1,) + (1,) * (len(shape) - position - 1))

    gain = one(*shards[0])
    for cut in shards[1:]:
        gain = gain * one(*cut)
    return gain


def bell_draw(key, dims, spread, bound, cuts=(), kind=jnp.bfloat16):
    loudness = level_of(key, dims, cuts, -0.22, 0.18) if cuts else 1.0
    values = jax.random.normal(key, dims, jnp.float32) * spread * loudness
    return jnp.minimum(jnp.maximum(values, -bound), bound).astype(kind)


def setup_inputs(seed: int = 0) -> dict:
    keys = jax.random.split(jax.random.key(seed), 9)
    query_input = bell_draw(keys[0], (SEQ_LEN, C), 1.0, 6.0, ((0, 64), (1, 4)))
    key_input = bell_draw(keys[1], (SEQ_LEN, C), 1.0, 6.0, ((0, 64), (1, 4)))
    value_input = bell_draw(keys[2], (SEQ_LEN, C), 1.0, 6.0, ((0, 64), (1, 4)))
    short_filter = bell_draw(keys[3], (3, 3, C), 0.6, 3.0, ((2, 4),), jnp.float32)
    residues = bell_draw(keys[4], (ORDER, C), 0.25, 1.5, ((1, 4),), jnp.float32)
    decays = draw_decays(jax.random.fold_in(keys[8], 71), 0)
    skip_gain = bell_draw(keys[6], (C,), 1.0, 4.0, ((0, 4),), jnp.float32)
    head_weight = bell_draw(keys[7], (KERNEL, C, OUT), (KERNEL * C) ** -0.5, 0.015625, ((1, 256),))
    return dict(query_input=query_input, key_input=key_input, value_input=value_input, short_filter=short_filter, residues=residues, decays=decays, skip_gain=skip_gain, head_weight=head_weight)


channel_block = 128

def short_pass(signal, tap_weights):
    values = signal.astype(jnp.float32)
    row_count = values.shape[0]
    padded = jnp.pad(values, ((2, 0), (0, 0)))
    return tap_weights[0] * padded[2:2 + row_count] + tap_weights[1] * padded[1:1 + row_count] + tap_weights[2] * padded[0:row_count]

def long_block(gated, residue_block, decay_block):
    length = gated.shape[0]
    step_axis = jnp.arange(length, dtype=jnp.float32)[:, None]

    def add_mode(running, mode_pair):
        residue_row, decay_row = mode_pair
        weight_row = residue_row * jnp.sqrt(-jnp.expm1(-2.0 * decay_row))
        return (running + weight_row[None, :] * jnp.exp(-decay_row[None, :] * step_axis), None)
    filters = lax.scan(add_mode, jnp.zeros(gated.shape, jnp.float32), (residue_block, decay_block))[0]
    spectrum = jnp.fft.rfft(filters, n=2 * length, axis=0) * jnp.fft.rfft(gated.astype(jnp.float32), n=2 * length, axis=0)
    return jnp.fft.irfft(spectrum, n=2 * length, axis=0)[:length].astype(jnp.float32)

def reference(query_input, key_input, value_input, short_filter, residues, decays, skip_gain, head_weight):

    def chain_block(block_index):
        block_start = (block_index * channel_block).astype(jnp.int32)

        def take_block(array):
            return lax.dynamic_slice_in_dim(array, block_start, channel_block, array.ndim - 1)
        tap_weights = take_block(short_filter)
        query_short = short_pass(take_block(query_input), tap_weights[:, 0])
        key_short = short_pass(take_block(key_input), tap_weights[:, 1])
        value_short = short_pass(take_block(value_input), tap_weights[:, 2])
        gated = (key_short * value_short).astype(jnp.bfloat16)
        convolved = long_block(gated, take_block(residues), take_block(decays))
        carried = (convolved + take_block(skip_gain)[None, :] * gated.astype(jnp.float32)).astype(jnp.bfloat16)
        return (query_short * carried.astype(jnp.float32)).astype(jnp.bfloat16)
    blocks = lax.map(chain_block, jnp.arange(C // channel_block, dtype=jnp.int32))
    operator_out = jnp.transpose(blocks, (1, 0, 2)).reshape(SEQ_LEN, C)
    extended = jnp.concatenate([operator_out, jnp.zeros((STRIDE, C), jnp.bfloat16)], axis=0)
    extended = extended.reshape(SEQ_LEN // STRIDE + 1, STRIDE * C)
    early_taps = head_weight[:STRIDE].reshape(STRIDE * C, OUT)
    late_taps = head_weight[STRIDE:].reshape(STRIDE * C, OUT)
    probe_sum = jnp.dot(extended[:-1], early_taps, preferred_element_type=jnp.float32) + jnp.dot(extended[1:], late_taps, preferred_element_type=jnp.float32)
    return (operator_out, probe_sum.astype(jnp.bfloat16))
```

```python
import jax
import jax.numpy as jnp
from jax import lax
from jax.sharding import PartitionSpec as P

STRIDE = 16

highest = lax.Precision.HIGHEST


def from_behind(block, axis, distance):
    devices = range(lax.axis_size(axis))
    route = [(i - distance, i) for i in devices if i - distance in devices]
    return lax.ppermute(block, axis, route)


def short_pass(rows_block, before, tap_weights):
    joined = jnp.concatenate([before, rows_block], axis=0).astype(jnp.float32)
    row_count = rows_block.shape[0]
    return (
        tap_weights[0] * joined[2 : 2 + row_count]
        + tap_weights[1] * joined[1 : 1 + row_count]
        + tap_weights[2] * joined[0:row_count]
    )


def modal_conv(gated, residues, decays):
    tokens = gated.shape[0]
    parties = lax.axis_size("seq")
    g = gated.astype(jnp.float32)
    steps = jnp.arange(tokens, dtype=jnp.float32)
    weight = residues * jnp.sqrt(-jnp.expm1(-2.0 * decays))
    grow = jnp.exp(decays[:, None, :] * steps[None, :, None])
    shrink = jnp.exp(-decays[:, None, :] * steps[None, :, None])
    lower = (steps[:, None] >= steps[None, :]).astype(jnp.float32)
    running = jnp.einsum("ij,rjc->ric", lower, grow * g[None], precision=highest)
    local = jnp.sum(weight[:, None, :] * shrink * running, axis=0)
    end_state = jnp.exp(-decays * (tokens - 1)) * running[:, -1, :]
    carry = from_behind(end_state, "seq", 1)
    span = 1
    while span < parties:
        carry = carry + jnp.exp(-decays * float(tokens * span)) * from_behind(carry, "seq", span)
        span *= 2
    after = jnp.exp(-decays[:, None, :] * (steps[None, :, None] + 1.0))
    cross = jnp.sum((weight * carry)[:, None, :] * after, axis=0)
    return local + cross


def shards(
    query_input, key_input, value_input, short_filter, residues, decays, skip_gain, head_weight
):
    tokens, chan_width = query_input.shape
    before = from_behind((query_input[-2:], key_input[-2:], value_input[-2:]), "seq", 1)
    query_short = short_pass(query_input, before[0], short_filter[:, 0])
    key_short = short_pass(key_input, before[1], short_filter[:, 1])
    value_short = short_pass(value_input, before[2], short_filter[:, 2])
    gated = (key_short * value_short).astype(jnp.bfloat16)
    convolved = modal_conv(gated, residues, decays)
    carried = (convolved + skip_gain * gated.astype(jnp.float32)).astype(jnp.bfloat16)
    operator_out = (query_short * carried.astype(jnp.float32)).astype(jnp.bfloat16)
    rim_rows = from_behind(operator_out[:STRIDE], "seq", -1)
    extended = jnp.concatenate([operator_out, rim_rows], axis=0).reshape(
        tokens // STRIDE + 1, STRIDE, chan_width
    )
    early_rows = extended[:-1]
    late_rows = extended[1:]
    weight_piece = lax.all_gather(head_weight, "seq", axis=1, tiled=True)
    running = jnp.einsum(
        "jic,ico->jo", early_rows, weight_piece[:STRIDE], preferred_element_type=jnp.float32
    )
    partial_sum = running + jnp.einsum(
        "jic,ico->jo", late_rows, weight_piece[STRIDE:], preferred_element_type=jnp.float32
    )
    probe_out = lax.psum_scatter(partial_sum, "tp", scatter_dimension=0, tiled=True).astype(
        jnp.bfloat16
    )
    return (operator_out, probe_out)


def solution(mesh):
    placed = (
        P("seq", "tp"),
        P("seq", "tp"),
        P("seq", "tp"),
        P(None, None, "tp"),
        P(None, "tp"),
        P(None, "tp"),
        P("tp"),
        P(None, ("tp", "seq"), None),
    )
    return jax.shard_map(
        shards,
        mesh=mesh,
        in_specs=placed,
        out_specs=(P("seq", "tp"), P(("seq", "tp"), None)),
        check_vma=False,
    )
```

```python
import jax
import jax.numpy as jnp
from jax import lax
from jax.sharding import PartitionSpec as P

STRIDE = 16
RADIX = 8
SEQ = ("u", "v")

highest = lax.Precision.HIGHEST


def from_behind(block, axis, distance):
    devices = range(lax.axis_size(axis))
    route = [(i - distance, i) for i in devices if i - distance in devices]
    return lax.ppermute(block, axis, route)


def short_pass(rows_block, before, tap_weights):
    joined = jnp.concatenate([before, rows_block], axis=0).astype(jnp.float32)
    row_count = rows_block.shape[0]
    return (
        tap_weights[0] * joined[2 : 2 + row_count]
        + tap_weights[1] * joined[1 : 1 + row_count]
        + tap_weights[2] * joined[0:row_count]
    )


def shifted_sum(values, decays, tokens, stride):
    total = None
    for m in range(1, RADIX):
        term = from_behind(values, SEQ, stride * m)
        if m > 1:
            term = jnp.exp(-decays * float(tokens * stride * (m - 1))) * term
        total = term if total is None else total + term
    return total


def modal_conv(gated, residues, decays):
    tokens = gated.shape[0]
    parties = lax.axis_size(SEQ)
    g = gated.astype(jnp.float32)
    steps = jnp.arange(tokens, dtype=jnp.float32)
    weight = residues * jnp.sqrt(-jnp.expm1(-2.0 * decays))
    grow = jnp.exp(decays[:, None, :] * steps[None, :, None])
    shrink = jnp.exp(-decays[:, None, :] * steps[None, :, None])
    lower = (steps[:, None] >= steps[None, :]).astype(jnp.float32)
    running = jnp.einsum("ij,rjc->ric", lower, grow * g[None], precision=highest)
    local = jnp.sum(weight[:, None, :] * shrink * running, axis=0)
    end_state = jnp.exp(-decays * (tokens - 1)) * running[:, -1, :]
    carry = shifted_sum(end_state, decays, tokens, 1)
    inclusive = end_state + jnp.exp(-decays * float(tokens)) * carry
    carry = carry + jnp.exp(-decays * float(tokens * (RADIX - 1))) * shifted_sum(
        inclusive, decays, tokens, RADIX
    )
    after = jnp.exp(-decays[:, None, :] * (steps[None, :, None] + 1.0))
    cross = jnp.sum((weight * carry)[:, None, :] * after, axis=0)
    return local + cross


def shards(
    query_input, key_input, value_input, short_filter, residues, decays, skip_gain, head_weight
):
    tokens, chan_width = query_input.shape
    before = from_behind((query_input[-2:], key_input[-2:], value_input[-2:]), SEQ, 1)
    query_short = short_pass(query_input, before[0], short_filter[:, 0])
    key_short = short_pass(key_input, before[1], short_filter[:, 1])
    value_short = short_pass(value_input, before[2], short_filter[:, 2])
    gated = (key_short * value_short).astype(jnp.bfloat16)
    convolved = modal_conv(gated, residues, decays)
    carried = (convolved + skip_gain * gated.astype(jnp.float32)).astype(jnp.bfloat16)
    operator_out = (query_short * carried.astype(jnp.float32)).astype(jnp.bfloat16)
    rim_rows = from_behind(operator_out[:STRIDE], SEQ, -1)
    extended = jnp.concatenate([operator_out, rim_rows], axis=0)
    width_u = lax.axis_size("u")
    width_v = lax.axis_size("v")
    piece = head_weight.shape[1]
    parted = extended.reshape(tokens + STRIDE, width_u, width_v, piece)
    gathered = lax.all_to_all(parted, "v", split_axis=2, concat_axis=0, tiled=True)
    gathered = gathered.reshape(width_v, tokens + STRIDE, width_u * piece)
    weight_piece = lax.all_gather(head_weight, "u", axis=1, tiled=True)
    rows = tokens // STRIDE
    early_rows = gathered[:, :tokens].reshape(width_v, rows, STRIDE, width_u * piece)
    late_rows = gathered[:, STRIDE:].reshape(width_v, rows, STRIDE, width_u * piece)
    running = jnp.einsum(
        "bjic,ico->bjo", early_rows, weight_piece[:STRIDE], preferred_element_type=jnp.float32
    )
    partial_sum = running + jnp.einsum(
        "bjic,ico->bjo", late_rows, weight_piece[STRIDE:], preferred_element_type=jnp.float32
    )
    probe_out = lax.psum_scatter(
        partial_sum.reshape(width_v * rows, -1), ("v", "tp"), scatter_dimension=0, tiled=True
    ).astype(jnp.bfloat16)
    return (operator_out, probe_out)


def solution(mesh):
    placed = (
        P(SEQ, "tp"),
        P(SEQ, "tp"),
        P(SEQ, "tp"),
        P(None, None, "tp"),
        P(None, "tp"),
        P(None, "tp"),
        P("tp"),
        P(None, ("tp", "u", "v"), None),
    )
    seq_size, tp_size = mesh.devices.shape
    width_u = 4 if seq_size % 4 == 0 else 1
    split = jax.sharding.Mesh(
        mesh.devices.reshape(width_u, seq_size // width_u, tp_size), ("u", "v", "tp")
    )
    return jax.shard_map(
        shards,
        mesh=split,
        in_specs=placed,
        out_specs=(P(SEQ, "tp"), P(("u", "v", "tp"), None)),
        check_vma=False,
    )
```

```python
import jax
import jax.numpy as jnp
from jax import lax
from jax.sharding import PartitionSpec as P

STRIDE = 16
CHUNK = 128

highest = lax.Precision.HIGHEST


def from_behind(block, axis, distance):
    devices = range(lax.axis_size(axis))
    route = [(i - distance, i) for i in devices if i - distance in devices]
    return lax.ppermute(block, axis, route)


def short_pass(rows, before, tap_weights):
    joined = jnp.concatenate([before, rows], axis=0).astype(jnp.float32)
    row_count = rows.shape[0]
    return (
        tap_weights[0] * joined[2 : 2 + row_count]
        + tap_weights[1] * joined[1 : 1 + row_count]
        + tap_weights[2] * joined[0:row_count]
    )


def modal_conv(gated, residues, decays):
    span, width = gated.shape
    chunks = span // CHUNK
    groups = lax.axis_size("u")
    g = gated.astype(jnp.float32).reshape(chunks, CHUNK, width)
    steps = jnp.arange(CHUNK, dtype=jnp.float32)
    weight = residues * jnp.sqrt(-jnp.expm1(-2.0 * decays))
    grow = jnp.exp(decays[:, None, :] * steps[None, :, None])
    shrink = jnp.exp(-decays[:, None, :] * steps[None, :, None])
    lower = (steps[:, None] >= steps[None, :]).astype(jnp.float32)
    running = jnp.einsum("ij,rkjc->rkic", lower, grow[:, None] * g[None], precision=highest)
    ends = jnp.exp(-decays * (CHUNK - 1))[:, None, :] * running[:, :, -1, :]
    index = jnp.arange(chunks)
    lag = (index[:, None] - 1 - index[None, :]).astype(jnp.float32)
    decay_table = jnp.where(
        (lag >= 0)[None, :, :, None],
        jnp.exp(-decays[:, None, None, :] * (CHUNK * jnp.maximum(lag, 0.0))[None, :, :, None]),
        0.0,
    )
    inner = jnp.sum(decay_table * ends[:, None, :, :], axis=2)
    total = jnp.exp(-decays * CHUNK) * inner[:, -1] + ends[:, -1]
    outer = None
    for m in range(1, groups):
        term = from_behind(total, "u", m)
        if m > 1:
            term = jnp.exp(-decays * float(span * (m - 1))) * term
        outer = term if outer is None else outer + term
    if outer is not None:
        offsets = (CHUNK * index).astype(jnp.float32)
        inner = inner + jnp.exp(-decays[:, None, :] * offsets[None, :, None]) * outer[:, None, :]
    after = jnp.exp(-decays[:, None, :] * (steps[None, :, None] + 1.0))
    modes = shrink[:, None] * running + after[:, None] * inner[:, :, None, :]
    return jnp.sum(weight[:, None, None, :] * modes, axis=0).reshape(span, width)


def shards(
    query_input, key_input, value_input, short_filter, residues, decays, skip_gain, head_weight
):
    tokens, chan_width = query_input.shape
    width_u = lax.axis_size("u")
    width_v = lax.axis_size("v")
    piece = head_weight.shape[1]
    span = tokens * width_v
    narrow = width_u * piece
    stacked = jnp.stack([query_input, key_input, value_input], axis=0)
    stacked = stacked.reshape(1, 3, tokens, width_u, width_v, piece)
    columns = lax.all_to_all(stacked, "v", split_axis=4, concat_axis=0, tiled=True)
    columns = columns.reshape(width_v, 3, tokens, narrow)
    columns = jnp.transpose(columns, (1, 0, 2, 3)).reshape(3, span, narrow)
    weight_rep = jnp.broadcast_to(head_weight[None], (width_u,) + head_weight.shape)
    weight_cols = lax.all_to_all(weight_rep, "u", split_axis=0, concat_axis=0, tiled=True)
    weight_cols = jnp.transpose(weight_cols, (1, 0, 2, 3)).reshape(
        head_weight.shape[0], narrow, head_weight.shape[2]
    )
    before = from_behind(columns[:, -2:], "u", 1)
    sf = short_filter.reshape(3, 3, width_u, width_v, piece)
    sf = jnp.transpose(sf, (0, 1, 3, 2, 4))
    sf = lax.dynamic_index_in_dim(sf, lax.axis_index("v"), axis=2, keepdims=False)
    sf = sf.reshape(3, 3, narrow)

    def pick(values):
        shaped = values.reshape(values.shape[0], width_u, width_v, piece)
        shaped = lax.dynamic_index_in_dim(shaped, lax.axis_index("v"), axis=2, keepdims=False)
        return shaped.reshape(values.shape[0], narrow)

    query_short = short_pass(columns[0], before[0], sf[:, 0])
    key_short = short_pass(columns[1], before[1], sf[:, 1])
    value_short = short_pass(columns[2], before[2], sf[:, 2])
    gated = (key_short * value_short).astype(jnp.bfloat16)
    convolved = modal_conv(gated, pick(residues), pick(decays))
    gain = pick(skip_gain[None])[0]
    carried = (convolved + gain * gated.astype(jnp.float32)).astype(jnp.bfloat16)
    op_cols = (query_short * carried.astype(jnp.float32)).astype(jnp.bfloat16)
    back = op_cols.reshape(width_v, tokens, width_u, 1, piece)
    back = lax.all_to_all(back, "v", split_axis=0, concat_axis=3, tiled=True)
    operator_out = back.reshape(tokens, chan_width)
    rim_rows = from_behind(op_cols[:STRIDE], "u", -1)
    extended = jnp.concatenate([op_cols, rim_rows], axis=0)
    rows = span // STRIDE
    early_rows = extended[:span].reshape(rows, STRIDE, narrow)
    late_rows = extended[STRIDE:].reshape(rows, STRIDE, narrow)
    running = jnp.einsum(
        "jic,ico->jo", early_rows, weight_cols[:STRIDE], preferred_element_type=jnp.float32
    )
    partial_sum = running + jnp.einsum(
        "jic,ico->jo", late_rows, weight_cols[STRIDE:], preferred_element_type=jnp.float32
    )
    partial_sum = partial_sum.reshape(width_v, rows // width_v, -1)
    partial_sum = lax.all_to_all(partial_sum, "v", split_axis=0, concat_axis=0, tiled=True)
    block_sum = jnp.sum(partial_sum, axis=0)
    probe_out = lax.psum_scatter(block_sum, "tp", scatter_dimension=0, tiled=True).astype(
        jnp.bfloat16
    )
    return (operator_out, probe_out)


def solution(mesh):
    seq_size, tp_size = mesh.devices.shape
    width_u = 4 if seq_size % 4 == 0 else 1
    split = jax.sharding.Mesh(
        mesh.devices.reshape(width_u, seq_size // width_u, tp_size), ("u", "v", "tp")
    )
    seq = ("u", "v")
    placed = (
        P(seq, "tp"),
        P(seq, "tp"),
        P(seq, "tp"),
        P(None, None, "tp"),
        P(None, "tp"),
        P(None, "tp"),
        P("tp"),
        P(None, ("tp", "u", "v"), None),
    )
    return jax.shard_map(
        shards,
        mesh=split,
        in_specs=placed,
        out_specs=(P(seq, "tp"), P(("u", "v", "tp"), None)),
        check_vma=False,
    )
```

```python
import jax
import jax.numpy as jnp
from jax import lax
from jax.experimental import pallas as pl
from jax.sharding import PartitionSpec as P

STRIDE = 16
CHUNK = 128
INTERPRET = False

highest = lax.Precision.HIGHEST


def from_behind(block, axis, distance):
    devices = range(lax.axis_size(axis))
    route = [(i - distance, i) for i in devices if i - distance in devices]
    return lax.ppermute(block, axis, route)


def short_pass(rows, before, tap_weights):
    joined = jnp.concatenate([before, rows], axis=0).astype(jnp.float32)
    row_count = rows.shape[0]
    return (
        tap_weights[0] * joined[2 : 2 + row_count]
        + tap_weights[1] * joined[1 : 1 + row_count]
        + tap_weights[2] * joined[0:row_count]
    )


def conv_kernel(g_ref, d_ref, w_ref, out_ref, total_ref):
    span, width = g_ref.shape
    chunks = span // CHUNK
    row = lax.broadcasted_iota(jnp.int32, (CHUNK, CHUNK), 0)
    col = lax.broadcasted_iota(jnp.int32, (CHUNK, CHUNK), 1)
    lower = (row >= col).astype(jnp.float32)
    steps = lax.broadcasted_iota(jnp.int32, (CHUNK, width), 0).astype(jnp.float32)
    out_ref[...] = jnp.zeros(out_ref.shape, jnp.float32)

    def mode(r, carry):
        d = d_ref[pl.ds(r, 1), :]
        w = w_ref[pl.ds(r, 1), :]
        grow = jnp.exp(d * steps)
        shrink = w * jnp.exp(-d * steps)
        after = w * jnp.exp(-d * (steps + 1.0))
        tail = jnp.exp(-d * float(CHUNK - 1))
        hop = jnp.exp(-d * float(CHUNK))
        state = jnp.zeros((1, width), jnp.float32)
        for k in range(chunks):
            rows = slice(k * CHUNK, (k + 1) * CHUNK)
            y = jnp.dot(
                lower, grow * g_ref[rows, :], precision=highest,
                preferred_element_type=jnp.float32,
            )
            out_ref[rows, :] += shrink * y + after * state
            state = hop * state + tail * y[CHUNK - 1 : CHUNK, :]
        total_ref[pl.ds(r, 1), :] = state
        return carry

    lax.fori_loop(0, d_ref.shape[0], mode, 0)


def modal_conv(gated, residues, decays):
    span, width = gated.shape
    groups = lax.axis_size("u")
    weight = residues * jnp.sqrt(-jnp.expm1(-2.0 * decays))
    local, total = pl.pallas_call(
        conv_kernel,
        out_shape=(
            jax.ShapeDtypeStruct((span, width), jnp.float32),
            jax.ShapeDtypeStruct(decays.shape, jnp.float32),
        ),
        interpret=INTERPRET,
    )(gated.astype(jnp.float32), decays, weight)
    outer = None
    for m in range(1, groups):
        term = from_behind(total, "u", m)
        if m > 1:
            term = jnp.exp(-decays * float(span * (m - 1))) * term
        outer = term if outer is None else outer + term
    if outer is None:
        return local
    steps = jnp.arange(span, dtype=jnp.float32)
    after = jnp.exp(-decays[:, None, :] * (steps[None, :, None] + 1.0))
    return local + jnp.sum((weight * outer)[:, None, :] * after, axis=0)


def shards(
    query_input, key_input, value_input, short_filter, residues, decays, skip_gain, head_weight
):
    tokens, chan_width = query_input.shape
    width_u = lax.axis_size("u")
    width_v = lax.axis_size("v")
    piece = head_weight.shape[1]
    span = tokens * width_v
    narrow = width_u * piece
    def columns_of(values):
        parted = values.reshape(1, tokens, width_u, width_v, piece)
        moved = lax.all_to_all(parted, "v", split_axis=3, concat_axis=0, tiled=True)
        return moved.reshape(span, narrow)

    columns = [columns_of(x) for x in (key_input, value_input, query_input)]
    weight_rep = jnp.broadcast_to(head_weight[None], (width_u,) + head_weight.shape)
    weight_cols = lax.all_to_all(weight_rep, "u", split_axis=0, concat_axis=0, tiled=True)
    weight_cols = jnp.transpose(weight_cols, (1, 0, 2, 3)).reshape(
        head_weight.shape[0], narrow, head_weight.shape[2]
    )
    before = from_behind(tuple(x[-2:] for x in columns), "u", 1)
    sf = short_filter.reshape(3, 3, width_u, width_v, piece)
    sf = jnp.transpose(sf, (0, 1, 3, 2, 4))
    sf = lax.dynamic_index_in_dim(sf, lax.axis_index("v"), axis=2, keepdims=False)
    sf = sf.reshape(3, 3, narrow)

    def pick(values):
        shaped = values.reshape(values.shape[0], width_u, width_v, piece)
        shaped = lax.dynamic_index_in_dim(shaped, lax.axis_index("v"), axis=2, keepdims=False)
        return shaped.reshape(values.shape[0], narrow)

    key_short = short_pass(columns[0], before[0], sf[:, 1])
    value_short = short_pass(columns[1], before[1], sf[:, 2])
    query_short = short_pass(columns[2], before[2], sf[:, 0])
    gated = (key_short * value_short).astype(jnp.bfloat16)
    convolved = modal_conv(gated, pick(residues), pick(decays))
    gain = pick(skip_gain[None])[0]
    carried = (convolved + gain * gated.astype(jnp.float32)).astype(jnp.bfloat16)
    op_cols = (query_short * carried.astype(jnp.float32)).astype(jnp.bfloat16)
    back = op_cols.reshape(width_v, tokens, width_u, 1, piece)
    back = lax.all_to_all(back, "v", split_axis=0, concat_axis=3, tiled=True)
    operator_out = back.reshape(tokens, chan_width)
    rim_rows = from_behind(op_cols[:STRIDE], "u", -1)
    extended = jnp.concatenate([op_cols, rim_rows], axis=0)
    rows = span // STRIDE
    early_rows = extended[:span].reshape(rows, STRIDE, narrow)
    late_rows = extended[STRIDE:].reshape(rows, STRIDE, narrow)
    running = jnp.einsum(
        "jic,ico->jo", early_rows, weight_cols[:STRIDE], preferred_element_type=jnp.float32
    )
    partial_sum = running + jnp.einsum(
        "jic,ico->jo", late_rows, weight_cols[STRIDE:], preferred_element_type=jnp.float32
    )
    partial_sum = partial_sum.reshape(width_v, rows // width_v, -1)
    partial_sum = lax.all_to_all(partial_sum, "v", split_axis=0, concat_axis=0, tiled=True)
    block_sum = jnp.sum(partial_sum, axis=0)
    probe_out = lax.psum_scatter(block_sum, "tp", scatter_dimension=0, tiled=True).astype(
        jnp.bfloat16
    )
    return (operator_out, probe_out)


def solution(mesh):
    seq_size, tp_size = mesh.devices.shape
    width_u = 4 if seq_size % 4 == 0 else 1
    split = jax.sharding.Mesh(
        mesh.devices.reshape(width_u, seq_size // width_u, tp_size), ("u", "v", "tp")
    )
    seq = ("u", "v")
    placed = (
        P(seq, "tp"),
        P(seq, "tp"),
        P(seq, "tp"),
        P(None, None, "tp"),
        P(None, "tp"),
        P(None, "tp"),
        P("tp"),
        P(None, ("tp", "u", "v"), None),
    )
    return jax.shard_map(
        shards,
        mesh=split,
        in_specs=placed,
        out_specs=(P(seq, "tp"), P(("u", "v", "tp"), None)),
        check_vma=False,
    )
```

```python
import jax
import jax.numpy as jnp
from jax import lax
from jax.experimental import pallas as pl
from jax.sharding import PartitionSpec as P

STRIDE = 16
CHUNK = 128
INTERPRET = False

highest = lax.Precision.HIGHEST


def from_behind(block, axis, distance):
    devices = range(lax.axis_size(axis))
    route = [(i - distance, i) for i in devices if i - distance in devices]
    return lax.ppermute(block, axis, route)


def short_pass(rows, before, tap_weights):
    joined = jnp.concatenate([before, rows], axis=0).astype(jnp.float32)
    row_count = rows.shape[0]
    return (
        tap_weights[0] * joined[2 : 2 + row_count]
        + tap_weights[1] * joined[1 : 1 + row_count]
        + tap_weights[2] * joined[0:row_count]
    )


def conv_kernel(g_ref, d_ref, w_ref, out_ref, total_ref):
    span, width = g_ref.shape
    chunks = span // CHUNK
    row = lax.broadcasted_iota(jnp.int32, (CHUNK, CHUNK), 0)
    col = lax.broadcasted_iota(jnp.int32, (CHUNK, CHUNK), 1)
    lower = (row >= col).astype(jnp.bfloat16)
    steps = lax.broadcasted_iota(jnp.int32, (CHUNK, width), 0).astype(jnp.float32)
    out_ref[...] = jnp.zeros(out_ref.shape, jnp.float32)

    def mode(r, carry):
        d = d_ref[pl.ds(r, 1), :]
        w = w_ref[pl.ds(r, 1), :]
        grow = jnp.exp(d * steps)
        shrink = w * jnp.exp(-d * steps)
        after = w * jnp.exp(-d * (steps + 1.0))
        tail = jnp.exp(-d * float(CHUNK - 1))
        hop = jnp.exp(-d * float(CHUNK))
        state = jnp.zeros((1, width), jnp.float32)
        for k in range(chunks):
            rows = slice(k * CHUNK, (k + 1) * CHUNK)
            scaled = grow * g_ref[rows, :]
            high = scaled.astype(jnp.bfloat16)
            low = (scaled - high.astype(jnp.float32)).astype(jnp.bfloat16)
            y = jnp.dot(lower, high, preferred_element_type=jnp.float32) + jnp.dot(
                lower, low, preferred_element_type=jnp.float32
            )
            out_ref[rows, :] += shrink * y + after * state
            state = hop * state + tail * y[CHUNK - 1 : CHUNK, :]
        total_ref[pl.ds(r, 1), :] = state
        return carry

    lax.fori_loop(0, d_ref.shape[0], mode, 0)


def modal_conv(gated, residues, decays):
    span, width = gated.shape
    half = span // 2
    groups = lax.axis_size("u")
    weight = residues * jnp.sqrt(-jnp.expm1(-2.0 * decays))
    g = gated.astype(jnp.float32)
    packed = jnp.concatenate([g[:half], g[half:]], axis=1)
    decays2 = jnp.concatenate([decays, decays], axis=1)
    weight2 = jnp.concatenate([weight, weight], axis=1)
    local, ends = pl.pallas_call(
        conv_kernel,
        out_shape=(
            jax.ShapeDtypeStruct((half, 2 * width), jnp.float32),
            jax.ShapeDtypeStruct(decays2.shape, jnp.float32),
        ),
        interpret=INTERPRET,
    )(packed, decays2, weight2)
    hop_half = jnp.exp(-decays * float(half))
    first_end, second_end = ends[:, :width], ends[:, width:]
    total = hop_half * first_end + second_end
    outer = None
    for m in range(1, groups):
        term = from_behind(total, "u", m)
        if m > 1:
            term = jnp.exp(-decays * float(span * (m - 1))) * term
        outer = term if outer is None else outer + term
    if outer is None:
        entry = jnp.concatenate([jnp.zeros_like(first_end), first_end], axis=1)
    else:
        entry = jnp.concatenate([outer, hop_half * outer + first_end], axis=1)
    steps = jnp.arange(half, dtype=jnp.float32)
    after = jnp.exp(-decays2[:, None, :] * (steps[None, :, None] + 1.0))
    joined = local + jnp.sum((weight2 * entry)[:, None, :] * after, axis=0)
    return jnp.concatenate([joined[:, :width], joined[:, width:]], axis=0)


def shards(
    query_input, key_input, value_input, short_filter, residues, decays, skip_gain, head_weight
):
    tokens, chan_width = query_input.shape
    width_u = lax.axis_size("u")
    width_v = lax.axis_size("v")
    piece = head_weight.shape[1]
    span = tokens * width_v
    narrow = width_u * piece
    stacked = jnp.stack([key_input, value_input, query_input], axis=0)
    stacked = stacked.reshape(1, 3, tokens, width_u, width_v, piece)
    columns = lax.all_to_all(stacked, "v", split_axis=4, concat_axis=0, tiled=True)
    columns = columns.reshape(width_v, 3, tokens, narrow)
    columns = jnp.transpose(columns, (1, 0, 2, 3)).reshape(3, span, narrow)
    weight_rep = jnp.broadcast_to(head_weight[None], (width_u,) + head_weight.shape)
    weight_cols = lax.all_to_all(weight_rep, "u", split_axis=0, concat_axis=0, tiled=True)
    weight_cols = jnp.transpose(weight_cols, (1, 0, 2, 3)).reshape(
        head_weight.shape[0], narrow, head_weight.shape[2]
    )
    before = from_behind(columns[:, -2:], "u", 1)
    sf = short_filter.reshape(3, 3, width_u, width_v, piece)
    sf = jnp.transpose(sf, (0, 1, 3, 2, 4))
    sf = lax.dynamic_index_in_dim(sf, lax.axis_index("v"), axis=2, keepdims=False)
    sf = sf.reshape(3, 3, narrow)

    def pick(values):
        shaped = values.reshape(values.shape[0], width_u, width_v, piece)
        shaped = lax.dynamic_index_in_dim(shaped, lax.axis_index("v"), axis=2, keepdims=False)
        return shaped.reshape(values.shape[0], narrow)

    key_short = short_pass(columns[0], before[0], sf[:, 1])
    value_short = short_pass(columns[1], before[1], sf[:, 2])
    query_short = short_pass(columns[2], before[2], sf[:, 0])
    gated = (key_short * value_short).astype(jnp.bfloat16)
    convolved = modal_conv(gated, pick(residues), pick(decays))
    gain = pick(skip_gain[None])[0]
    carried = (convolved + gain * gated.astype(jnp.float32)).astype(jnp.bfloat16)
    op_cols = (query_short * carried.astype(jnp.float32)).astype(jnp.bfloat16)
    back = op_cols.reshape(width_v, tokens, width_u, 1, piece)
    back = lax.all_to_all(back, "v", split_axis=0, concat_axis=3, tiled=True)
    operator_out = back.reshape(tokens, chan_width)
    rim_rows = from_behind(op_cols[:STRIDE], "u", -1)
    extended = jnp.concatenate([op_cols, rim_rows], axis=0)
    rows = span // STRIDE
    early_rows = extended[:span].reshape(rows, STRIDE, narrow)
    late_rows = extended[STRIDE:].reshape(rows, STRIDE, narrow)
    running = jnp.einsum(
        "jic,ico->jo", early_rows, weight_cols[:STRIDE], preferred_element_type=jnp.float32
    )
    partial_sum = running + jnp.einsum(
        "jic,ico->jo", late_rows, weight_cols[STRIDE:], preferred_element_type=jnp.float32
    )
    partial_sum = partial_sum.reshape(width_v, rows // width_v, -1)
    partial_sum = lax.all_to_all(partial_sum, "v", split_axis=0, concat_axis=0, tiled=True)
    block_sum = jnp.sum(partial_sum, axis=0)
    probe_out = lax.psum_scatter(block_sum, "tp", scatter_dimension=0, tiled=True).astype(
        jnp.bfloat16
    )
    return (operator_out, probe_out)


def solution(mesh):
    seq_size, tp_size = mesh.devices.shape
    width_u = 4 if seq_size % 4 == 0 else 1
    split = jax.sharding.Mesh(
        mesh.devices.reshape(width_u, seq_size // width_u, tp_size), ("u", "v", "tp")
    )
    seq = ("u", "v")
    placed = (
        P(seq, "tp"),
        P(seq, "tp"),
        P(seq, "tp"),
        P(None, None, "tp"),
        P(None, "tp"),
        P(None, "tp"),
        P("tp"),
        P(None, ("tp", "u", "v"), None),
    )
    return jax.shard_map(
        shards,
        mesh=split,
        in_specs=placed,
        out_specs=(P(seq, "tp"), P(("u", "v", "tp"), None)),
        check_vma=False,
    )
```

```python
import jax
import jax.numpy as jnp
from jax import lax
from jax.experimental import pallas as pl
from jax.sharding import PartitionSpec as P

STRIDE = 16
CHUNK = 128
INTERPRET = False

highest = lax.Precision.HIGHEST


def from_behind(block, axis, distance):
    devices = range(lax.axis_size(axis))
    route = [(i - distance, i) for i in devices if i - distance in devices]
    return lax.ppermute(block, axis, route)


def short_pass(rows, before, tap_weights):
    joined = jnp.concatenate([before, rows], axis=0).astype(jnp.float32)
    row_count = rows.shape[0]
    return (
        tap_weights[0] * joined[2 : 2 + row_count]
        + tap_weights[1] * joined[1 : 1 + row_count]
        + tap_weights[2] * joined[0:row_count]
    )


def conv_kernel(g_ref, d_ref, w_ref, out_ref, total_ref):
    span, width = g_ref.shape
    chunks = span // CHUNK
    row = lax.broadcasted_iota(jnp.int32, (CHUNK, CHUNK), 0)
    col = lax.broadcasted_iota(jnp.int32, (CHUNK, CHUNK), 1)
    lower = (row >= col).astype(jnp.bfloat16)
    steps = lax.broadcasted_iota(jnp.int32, (CHUNK, width), 0).astype(jnp.float32)
    out_ref[...] = jnp.zeros(out_ref.shape, jnp.float32)

    def mode(r, carry):
        d = d_ref[pl.ds(r, 1), :]
        w = w_ref[pl.ds(r, 1), :]
        grow = jnp.exp(d * steps)
        shrink = w * jnp.exp(-d * steps)
        after = w * jnp.exp(-d * (steps + 1.0))
        tail = jnp.exp(-d * float(CHUNK - 1))
        hop = jnp.exp(-d * float(CHUNK))
        state = jnp.zeros((1, width), jnp.float32)
        for k in range(chunks):
            rows = slice(k * CHUNK, (k + 1) * CHUNK)
            scaled = grow * g_ref[rows, :]
            high = scaled.astype(jnp.bfloat16)
            low = (scaled - high.astype(jnp.float32)).astype(jnp.bfloat16)
            y = jnp.dot(lower, high, preferred_element_type=jnp.float32) + jnp.dot(
                lower, low, preferred_element_type=jnp.float32
            )
            out_ref[rows, :] += shrink * y + after * state
            state = hop * state + tail * y[CHUNK - 1 : CHUNK, :]
        total_ref[pl.ds(r, 1), :] = state
        return carry

    lax.fori_loop(0, d_ref.shape[0], mode, 0)


def modal_conv(gated, residues, decays):
    span, width = gated.shape
    half = span // 2
    groups = lax.axis_size("u")
    weight = residues * jnp.sqrt(-jnp.expm1(-2.0 * decays))
    g = gated.astype(jnp.float32)
    packed = jnp.concatenate([g[:half], g[half:]], axis=1)
    decays2 = jnp.concatenate([decays, decays], axis=1)
    weight2 = jnp.concatenate([weight, weight], axis=1)
    local, ends = pl.pallas_call(
        conv_kernel,
        out_shape=(
            jax.ShapeDtypeStruct((half, 2 * width), jnp.float32),
            jax.ShapeDtypeStruct(decays2.shape, jnp.float32),
        ),
        interpret=INTERPRET,
    )(packed, decays2, weight2)
    hop_half = jnp.exp(-decays * float(half))
    first_end, second_end = ends[:, :width], ends[:, width:]
    total = hop_half * first_end + second_end
    outer = None
    for m in range(1, groups):
        term = from_behind(total, "u", m)
        if m > 1:
            term = jnp.exp(-decays * float(span * (m - 1))) * term
        outer = term if outer is None else outer + term
    if outer is None:
        entry = jnp.concatenate([jnp.zeros_like(first_end), first_end], axis=1)
    else:
        entry = jnp.concatenate([outer, hop_half * outer + first_end], axis=1)
    steps = jnp.arange(half, dtype=jnp.float32)
    after = jnp.exp(-decays2[:, None, :] * (steps[None, :, None] + 1.0))
    joined = local + jnp.sum((weight2 * entry)[:, None, :] * after, axis=0)
    return jnp.concatenate([joined[:, :width], joined[:, width:]], axis=0)


def shards(
    query_input, key_input, value_input, short_filter, residues, decays, skip_gain, head_weight
):
    tokens, chan_width = query_input.shape
    width_u = lax.axis_size("u")
    width_v = lax.axis_size("v")
    piece = head_weight.shape[1]
    span = tokens * width_v
    narrow = width_u * piece
    before = from_behind(
        jnp.stack([query_input[-2:], key_input[-2:], value_input[-2:]], axis=0), ("u", "v"), 1
    )
    key_short = short_pass(key_input, before[1], short_filter[:, 1])
    value_short = short_pass(value_input, before[2], short_filter[:, 2])
    gated_rows = (key_short * value_short).astype(jnp.bfloat16)
    payload = jnp.concatenate([before[0], query_input, gated_rows], axis=0)
    depth = payload.shape[0]
    payload = payload.reshape(1, depth, width_u, width_v, piece)
    columns = lax.all_to_all(payload, "v", split_axis=3, concat_axis=0, tiled=True)
    columns = columns.reshape(width_v, depth, narrow)
    query_before = columns[0, :2]
    query_cols = columns[:, 2 : 2 + tokens].reshape(span, narrow)
    gated = columns[:, 2 + tokens :].reshape(span, narrow)
    head_weight, gated = lax.optimization_barrier((head_weight, gated))
    weight_rep = jnp.broadcast_to(head_weight[None], (width_u,) + head_weight.shape)
    weight_cols = lax.all_to_all(weight_rep, "u", split_axis=0, concat_axis=0, tiled=True)
    weight_cols = jnp.transpose(weight_cols, (1, 0, 2, 3)).reshape(
        head_weight.shape[0], narrow, head_weight.shape[2]
    )
    sf = short_filter.reshape(3, 3, width_u, width_v, piece)
    sf = jnp.transpose(sf, (0, 1, 3, 2, 4))
    sf = lax.dynamic_index_in_dim(sf, lax.axis_index("v"), axis=2, keepdims=False)
    sf = sf.reshape(3, 3, narrow)

    def pick(values):
        shaped = values.reshape(values.shape[0], width_u, width_v, piece)
        shaped = lax.dynamic_index_in_dim(shaped, lax.axis_index("v"), axis=2, keepdims=False)
        return shaped.reshape(values.shape[0], narrow)

    query_short = short_pass(query_cols, query_before, sf[:, 0])
    convolved = modal_conv(gated, pick(residues), pick(decays))
    gain = pick(skip_gain[None])[0]
    carried = (convolved + gain * gated.astype(jnp.float32)).astype(jnp.bfloat16)
    op_cols = (query_short * carried.astype(jnp.float32)).astype(jnp.bfloat16)
    rim_rows = from_behind(op_cols[:STRIDE], "u", -1)
    extended = jnp.concatenate([op_cols, rim_rows], axis=0)
    rows = span // STRIDE
    early_rows = extended[:span].reshape(rows, STRIDE, narrow)
    late_rows = extended[STRIDE:].reshape(rows, STRIDE, narrow)
    running = jnp.einsum(
        "jic,ico->jo", early_rows, weight_cols[:STRIDE], preferred_element_type=jnp.float32
    )
    partial_sum = running + jnp.einsum(
        "jic,ico->jo", late_rows, weight_cols[STRIDE:], preferred_element_type=jnp.float32
    )
    outgoing = jnp.concatenate(
        [
            op_cols.reshape(width_v, tokens * narrow),
            partial_sum.astype(jnp.bfloat16).reshape(width_v, -1),
        ],
        axis=1,
    )
    incoming = lax.all_to_all(outgoing, "v", split_axis=0, concat_axis=0, tiled=True)
    back = incoming[:, : tokens * narrow].reshape(width_v, tokens, width_u, piece)
    operator_out = jnp.transpose(back, (1, 2, 0, 3)).reshape(tokens, chan_width)
    block_sum = jnp.sum(
        incoming[:, tokens * narrow :].astype(jnp.float32).reshape(width_v, rows // width_v, -1),
        axis=0,
    )
    probe_out = lax.psum_scatter(block_sum, "tp", scatter_dimension=0, tiled=True).astype(
        jnp.bfloat16
    )
    return (operator_out, probe_out)


def solution(mesh):
    seq_size, tp_size = mesh.devices.shape
    width_u = 4 if seq_size % 4 == 0 else 1
    split = jax.sharding.Mesh(
        mesh.devices.reshape(width_u, seq_size // width_u, tp_size), ("u", "v", "tp")
    )
    seq = ("u", "v")
    placed = (
        P(seq, "tp"),
        P(seq, "tp"),
        P(seq, "tp"),
        P(None, None, "tp"),
        P(None, "tp"),
        P(None, "tp"),
        P("tp"),
        P(None, ("tp", "u", "v"), None),
    )
    return jax.shard_map(
        shards,
        mesh=split,
        in_specs=placed,
        out_specs=(P(seq, "tp"), P(("u", "v", "tp"), None)),
        check_vma=False,
    )
```

```python
import jax
import jax.numpy as jnp
from jax import lax
from jax.experimental import pallas as pl
from jax.sharding import PartitionSpec as P

STRIDE = 16
CHUNK = 128
INTERPRET = False

highest = lax.Precision.HIGHEST


def from_behind(block, axis, distance):
    devices = range(lax.axis_size(axis))
    route = [(i - distance, i) for i in devices if i - distance in devices]
    return lax.ppermute(block, axis, route)


def short_pass(rows, before, tap_weights):
    joined = jnp.concatenate([before, rows], axis=0).astype(jnp.float32)
    row_count = rows.shape[0]
    return (
        tap_weights[0] * joined[2 : 2 + row_count]
        + tap_weights[1] * joined[1 : 1 + row_count]
        + tap_weights[2] * joined[0:row_count]
    )


def conv_kernel(g_ref, d_ref, w_ref, out_ref, total_ref):
    span, width = g_ref.shape
    chunks = span // CHUNK
    row = lax.broadcasted_iota(jnp.int32, (CHUNK, CHUNK), 0)
    col = lax.broadcasted_iota(jnp.int32, (CHUNK, CHUNK), 1)
    lower = (row >= col).astype(jnp.bfloat16)
    steps = lax.broadcasted_iota(jnp.int32, (CHUNK, width), 0).astype(jnp.float32)
    out_ref[...] = jnp.zeros(out_ref.shape, jnp.float32)

    def mode(r, carry):
        d = d_ref[pl.ds(r, 1), :]
        w = w_ref[pl.ds(r, 1), :]
        grow = jnp.exp(d * steps)
        shrink = w * jnp.exp(-d * steps)
        after = w * jnp.exp(-d * (steps + 1.0))
        tail = jnp.exp(-d * float(CHUNK - 1))
        hop = jnp.exp(-d * float(CHUNK))
        state = jnp.zeros((1, width), jnp.float32)
        for k in range(chunks):
            rows = slice(k * CHUNK, (k + 1) * CHUNK)
            scaled = grow * g_ref[rows, :]
            high = scaled.astype(jnp.bfloat16)
            low = (scaled - high.astype(jnp.float32)).astype(jnp.bfloat16)
            y = jnp.dot(lower, high, preferred_element_type=jnp.float32) + jnp.dot(
                lower, low, preferred_element_type=jnp.float32
            )
            out_ref[rows, :] += shrink * y + after * state
            state = hop * state + tail * y[CHUNK - 1 : CHUNK, :]
        total_ref[pl.ds(r, 1), :] = state
        return carry

    lax.fori_loop(0, d_ref.shape[0], mode, 0)


def modal_conv(gated, residues, decays):
    span, width = gated.shape
    half = span // 2
    groups = lax.axis_size("u")
    weight = residues * jnp.sqrt(-jnp.expm1(-2.0 * decays))
    g = gated.astype(jnp.float32)
    packed = jnp.concatenate([g[:half], g[half:]], axis=1)
    decays2 = jnp.concatenate([decays, decays], axis=1)
    weight2 = jnp.concatenate([weight, weight], axis=1)
    local, ends = pl.pallas_call(
        conv_kernel,
        out_shape=(
            jax.ShapeDtypeStruct((half, 2 * width), jnp.float32),
            jax.ShapeDtypeStruct(decays2.shape, jnp.float32),
        ),
        interpret=INTERPRET,
    )(packed, decays2, weight2)
    hop_half = jnp.exp(-decays * float(half))
    first_end, second_end = ends[:, :width], ends[:, width:]
    total = hop_half * first_end + second_end
    outer = None
    for m in range(1, groups):
        term = from_behind(total, "u", m)
        if m > 1:
            term = jnp.exp(-decays * float(span * (m - 1))) * term
        outer = term if outer is None else outer + term
    if outer is None:
        entry = jnp.concatenate([jnp.zeros_like(first_end), first_end], axis=1)
    else:
        entry = jnp.concatenate([outer, hop_half * outer + first_end], axis=1)
    steps = jnp.arange(half, dtype=jnp.float32)
    after = jnp.exp(-decays2[:, None, :] * (steps[None, :, None] + 1.0))
    joined = local + jnp.sum((weight2 * entry)[:, None, :] * after, axis=0)
    return jnp.concatenate([joined[:, :width], joined[:, width:]], axis=0)


def shards(
    query_input, key_input, value_input, short_filter, residues, decays, skip_gain, head_weight
):
    tokens, chan_width = query_input.shape
    width_u = lax.axis_size("u")
    width_v = lax.axis_size("v")
    piece = head_weight.shape[1]
    span = tokens * width_v
    narrow = width_u * piece
    before = from_behind(
        jnp.stack([query_input[-2:], key_input[-2:], value_input[-2:]], axis=0), ("u", "v"), 1
    )
    key_short = short_pass(key_input, before[1], short_filter[:, 1])
    value_short = short_pass(value_input, before[2], short_filter[:, 2])
    gated_rows = (key_short * value_short).astype(jnp.bfloat16)
    def columns_of(values):
        depth = values.shape[0]
        parted = values.reshape(1, depth, width_u, width_v, piece)
        moved = lax.all_to_all(parted, "v", split_axis=3, concat_axis=0, tiled=True)
        return moved.reshape(width_v, depth, narrow)

    gated = columns_of(gated_rows).reshape(span, narrow)
    query_rows = jnp.concatenate([before[0], query_input], axis=0)
    query_rows, gated = lax.optimization_barrier((query_rows, gated))
    columns = columns_of(query_rows)
    query_before = columns[0, :2]
    query_cols = columns[:, 2:].reshape(span, narrow)
    head_weight, gated = lax.optimization_barrier((head_weight, gated))
    weight_rep = jnp.broadcast_to(head_weight[None], (width_u,) + head_weight.shape)
    weight_cols = lax.all_to_all(weight_rep, "u", split_axis=0, concat_axis=0, tiled=True)
    weight_cols = jnp.transpose(weight_cols, (1, 0, 2, 3)).reshape(
        head_weight.shape[0], narrow, head_weight.shape[2]
    )
    sf = short_filter.reshape(3, 3, width_u, width_v, piece)
    sf = jnp.transpose(sf, (0, 1, 3, 2, 4))
    sf = lax.dynamic_index_in_dim(sf, lax.axis_index("v"), axis=2, keepdims=False)
    sf = sf.reshape(3, 3, narrow)

    def pick(values):
        shaped = values.reshape(values.shape[0], width_u, width_v, piece)
        shaped = lax.dynamic_index_in_dim(shaped, lax.axis_index("v"), axis=2, keepdims=False)
        return shaped.reshape(values.shape[0], narrow)

    query_short = short_pass(query_cols, query_before, sf[:, 0])
    convolved = modal_conv(gated, pick(residues), pick(decays))
    gain = pick(skip_gain[None])[0]
    carried = (convolved + gain * gated.astype(jnp.float32)).astype(jnp.bfloat16)
    op_cols = (query_short * carried.astype(jnp.float32)).astype(jnp.bfloat16)
    rim_rows = from_behind(op_cols[:STRIDE], "u", -1)
    extended = jnp.concatenate([op_cols, rim_rows], axis=0)
    rows = span // STRIDE
    early_rows = extended[:span].reshape(rows, STRIDE, narrow)
    late_rows = extended[STRIDE:].reshape(rows, STRIDE, narrow)
    running = jnp.einsum(
        "jic,ico->jo", early_rows, weight_cols[:STRIDE], preferred_element_type=jnp.float32
    )
    partial_sum = running + jnp.einsum(
        "jic,ico->jo", late_rows, weight_cols[STRIDE:], preferred_element_type=jnp.float32
    )
    outgoing = jnp.concatenate(
        [
            op_cols.reshape(width_v, tokens * narrow),
            partial_sum.astype(jnp.bfloat16).reshape(width_v, -1),
        ],
        axis=1,
    )
    incoming = lax.all_to_all(outgoing, "v", split_axis=0, concat_axis=0, tiled=True)
    back = incoming[:, : tokens * narrow].reshape(width_v, tokens, width_u, piece)
    operator_out = jnp.transpose(back, (1, 2, 0, 3)).reshape(tokens, chan_width)
    block_sum = jnp.sum(
        incoming[:, tokens * narrow :].astype(jnp.float32).reshape(width_v, rows // width_v, -1),
        axis=0,
    )
    probe_out = lax.psum_scatter(block_sum, "tp", scatter_dimension=0, tiled=True).astype(
        jnp.bfloat16
    )
    return (operator_out, probe_out)


def solution(mesh):
    seq_size, tp_size = mesh.devices.shape
    width_u = 4 if seq_size % 4 == 0 else 1
    split = jax.sharding.Mesh(
        mesh.devices.reshape(width_u, seq_size // width_u, tp_size), ("u", "v", "tp")
    )
    seq = ("u", "v")
    placed = (
        P(seq, "tp"),
        P(seq, "tp"),
        P(seq, "tp"),
        P(None, None, "tp"),
        P(None, "tp"),
        P(None, "tp"),
        P("tp"),
        P(None, ("tp", "u", "v"), None),
    )
    return jax.shard_map(
        shards,
        mesh=split,
        in_specs=placed,
        out_specs=(P(seq, "tp"), P(("u", "v", "tp"), None)),
        check_vma=False,
    )
```

```python
import jax
import jax.numpy as jnp
from jax import lax
from jax.experimental import pallas as pl
from jax.sharding import PartitionSpec as P

STRIDE = 16
CHUNK = 128
INTERPRET = False

highest = lax.Precision.HIGHEST


def from_behind(block, axis, distance):
    devices = range(lax.axis_size(axis))
    route = [(i - distance, i) for i in devices if i - distance in devices]
    return lax.ppermute(block, axis, route)


def short_pass(rows, before, tap_weights):
    joined = jnp.concatenate([before, rows], axis=0).astype(jnp.float32)
    row_count = rows.shape[0]
    return (
        tap_weights[0] * joined[2 : 2 + row_count]
        + tap_weights[1] * joined[1 : 1 + row_count]
        + tap_weights[2] * joined[0:row_count]
    )


def conv_kernel(g_ref, d_ref, w_ref, out_ref, total_ref):
    span, width = g_ref.shape
    chunks = span // CHUNK
    row = lax.broadcasted_iota(jnp.int32, (CHUNK, CHUNK), 0)
    col = lax.broadcasted_iota(jnp.int32, (CHUNK, CHUNK), 1)
    lower = (row >= col).astype(jnp.bfloat16)
    steps = lax.broadcasted_iota(jnp.int32, (CHUNK, width), 0).astype(jnp.float32)
    out_ref[...] = jnp.zeros(out_ref.shape, jnp.float32)

    def mode(r, carry):
        d = d_ref[pl.ds(r, 1), :]
        w = w_ref[pl.ds(r, 1), :]
        grow = jnp.exp(d * steps)
        shrink = w * jnp.exp(-d * steps)
        after = w * jnp.exp(-d * (steps + 1.0))
        tail = jnp.exp(-d * float(CHUNK - 1))
        hop = jnp.exp(-d * float(CHUNK))
        state = jnp.zeros((1, width), jnp.float32)
        for k in range(chunks):
            rows = slice(k * CHUNK, (k + 1) * CHUNK)
            scaled = grow * g_ref[rows, :]
            high = scaled.astype(jnp.bfloat16)
            low = (scaled - high.astype(jnp.float32)).astype(jnp.bfloat16)
            y = jnp.dot(lower, high, preferred_element_type=jnp.float32) + jnp.dot(
                lower, low, preferred_element_type=jnp.float32
            )
            out_ref[rows, :] += shrink * y + after * state
            state = hop * state + tail * y[CHUNK - 1 : CHUNK, :]
        total_ref[pl.ds(r, 1), :] = state
        return carry

    lax.fori_loop(0, d_ref.shape[0], mode, 0)


def modal_conv(gated, residues, decays):
    span, width = gated.shape
    half = span // 2
    groups = lax.axis_size("u")
    weight = residues * jnp.sqrt(-jnp.expm1(-2.0 * decays))
    g = gated.astype(jnp.float32)
    packed = jnp.concatenate([g[:half], g[half:]], axis=1)
    decays2 = jnp.concatenate([decays, decays], axis=1)
    weight2 = jnp.concatenate([weight, weight], axis=1)
    local, ends = pl.pallas_call(
        conv_kernel,
        out_shape=(
            jax.ShapeDtypeStruct((half, 2 * width), jnp.float32),
            jax.ShapeDtypeStruct(decays2.shape, jnp.float32),
        ),
        interpret=INTERPRET,
    )(packed, decays2, weight2)
    hop_half = jnp.exp(-decays * float(half))
    first_end, second_end = ends[:, :width], ends[:, width:]
    total = hop_half * first_end + second_end
    outer = None
    for m in range(1, groups):
        term = from_behind(total, "u", m)
        if m > 1:
            term = jnp.exp(-decays * float(span * (m - 1))) * term
        outer = term if outer is None else outer + term
    if outer is None:
        entry = jnp.concatenate([jnp.zeros_like(first_end), first_end], axis=1)
    else:
        entry = jnp.concatenate([outer, hop_half * outer + first_end], axis=1)
    steps = jnp.arange(half, dtype=jnp.float32)
    after = jnp.exp(-decays2[:, None, :] * (steps[None, :, None] + 1.0))
    joined = local + jnp.sum((weight2 * entry)[:, None, :] * after, axis=0)
    return jnp.concatenate([joined[:, :width], joined[:, width:]], axis=0)


def shards(
    query_input, key_input, value_input, short_filter, residues, decays, skip_gain, head_weight
):
    tokens, chan_width = query_input.shape
    width_u = lax.axis_size("u")
    width_v = lax.axis_size("v")
    piece = head_weight.shape[1]
    span = tokens * width_v
    narrow = width_u * piece
    before = from_behind(
        jnp.stack([query_input[-2:], key_input[-2:], value_input[-2:]], axis=0), ("u", "v"), 1
    )
    key_short = short_pass(key_input, before[1], short_filter[:, 1])
    value_short = short_pass(value_input, before[2], short_filter[:, 2])
    gated_rows = (key_short * value_short).astype(jnp.bfloat16)
    def columns_of(values):
        depth = values.shape[0]
        parted = values.reshape(1, depth, width_u, width_v, piece)
        moved = lax.all_to_all(parted, "v", split_axis=3, concat_axis=0, tiled=True)
        return moved.reshape(width_v, depth, narrow)

    gated = columns_of(gated_rows).reshape(span, narrow)
    query_rows = jnp.concatenate([before[0], query_input], axis=0)
    query_rows, gated = lax.optimization_barrier((query_rows, gated))
    columns = columns_of(query_rows)
    query_before = columns[0, :2]
    query_cols = columns[:, 2:].reshape(span, narrow)
    head_weight, query_cols = lax.optimization_barrier((head_weight, query_cols))
    weight_rep = jnp.broadcast_to(head_weight[None], (width_u,) + head_weight.shape)
    weight_cols = lax.all_to_all(weight_rep, "u", split_axis=0, concat_axis=0, tiled=True)
    weight_cols = jnp.transpose(weight_cols, (1, 0, 2, 3)).reshape(
        head_weight.shape[0], narrow, head_weight.shape[2]
    )
    sf = short_filter.reshape(3, 3, width_u, width_v, piece)
    sf = jnp.transpose(sf, (0, 1, 3, 2, 4))
    sf = lax.dynamic_index_in_dim(sf, lax.axis_index("v"), axis=2, keepdims=False)
    sf = sf.reshape(3, 3, narrow)

    def pick(values):
        shaped = values.reshape(values.shape[0], width_u, width_v, piece)
        shaped = lax.dynamic_index_in_dim(shaped, lax.axis_index("v"), axis=2, keepdims=False)
        return shaped.reshape(values.shape[0], narrow)

    query_short = short_pass(query_cols, query_before, sf[:, 0])
    convolved = modal_conv(gated, pick(residues), pick(decays))
    gain = pick(skip_gain[None])[0]
    carried = (convolved + gain * gated.astype(jnp.float32)).astype(jnp.bfloat16)
    op_cols = (query_short * carried.astype(jnp.float32)).astype(jnp.bfloat16)
    rim_rows = from_behind(op_cols[:STRIDE], "u", -1)
    extended = jnp.concatenate([op_cols, rim_rows], axis=0)
    rows = span // STRIDE
    early_rows = extended[:span].reshape(rows, STRIDE, narrow)
    late_rows = extended[STRIDE:].reshape(rows, STRIDE, narrow)
    running = jnp.einsum(
        "jic,ico->jo", early_rows, weight_cols[:STRIDE], preferred_element_type=jnp.float32
    )
    partial_sum = running + jnp.einsum(
        "jic,ico->jo", late_rows, weight_cols[STRIDE:], preferred_element_type=jnp.float32
    )
    outgoing = jnp.concatenate(
        [
            op_cols.reshape(width_v, tokens * narrow),
            partial_sum.astype(jnp.bfloat16).reshape(width_v, -1),
        ],
        axis=1,
    )
    incoming = lax.all_to_all(outgoing, "v", split_axis=0, concat_axis=0, tiled=True)
    back = incoming[:, : tokens * narrow].reshape(width_v, tokens, width_u, piece)
    operator_out = jnp.transpose(back, (1, 2, 0, 3)).reshape(tokens, chan_width)
    block_sum = jnp.sum(
        incoming[:, tokens * narrow :].astype(jnp.float32).reshape(width_v, rows // width_v, -1),
        axis=0,
    )
    probe_out = lax.psum_scatter(block_sum, "tp", scatter_dimension=0, tiled=True).astype(
        jnp.bfloat16
    )
    return (operator_out, probe_out)


def solution(mesh):
    seq_size, tp_size = mesh.devices.shape
    width_u = 4 if seq_size % 4 == 0 else 1
    split = jax.sharding.Mesh(
        mesh.devices.reshape(width_u, seq_size // width_u, tp_size), ("u", "v", "tp")
    )
    seq = ("u", "v")
    placed = (
        P(seq, "tp"),
        P(seq, "tp"),
        P(seq, "tp"),
        P(None, None, "tp"),
        P(None, "tp"),
        P(None, "tp"),
        P("tp"),
        P(None, ("tp", "u", "v"), None),
    )
    return jax.shard_map(
        shards,
        mesh=split,
        in_specs=placed,
        out_specs=(P(seq, "tp"), P(("u", "v", "tp"), None)),
        check_vma=False,
    )
```

```python
import jax
import jax.numpy as jnp
from jax import lax
from jax.experimental import pallas as pl
from jax.sharding import PartitionSpec as P

STRIDE = 16
CHUNK = 128
INTERPRET = False

highest = lax.Precision.HIGHEST


def from_behind(block, axis, distance):
    devices = range(lax.axis_size(axis))
    route = [(i - distance, i) for i in devices if i - distance in devices]
    return lax.ppermute(block, axis, route)


def short_pass(rows, before, tap_weights):
    joined = jnp.concatenate([before, rows], axis=0).astype(jnp.float32)
    row_count = rows.shape[0]
    return (
        tap_weights[0] * joined[2 : 2 + row_count]
        + tap_weights[1] * joined[1 : 1 + row_count]
        + tap_weights[2] * joined[0:row_count]
    )


def conv_kernel(g_ref, d_ref, w_ref, out_ref, total_ref):
    span, width = g_ref.shape
    chunks = span // CHUNK
    row = lax.broadcasted_iota(jnp.int32, (CHUNK, CHUNK), 0)
    col = lax.broadcasted_iota(jnp.int32, (CHUNK, CHUNK), 1)
    lower = (row >= col).astype(jnp.bfloat16)
    steps = lax.broadcasted_iota(jnp.int32, (CHUNK, width), 0).astype(jnp.float32)
    out_ref[...] = jnp.zeros(out_ref.shape, jnp.float32)

    def mode(r, carry):
        d = d_ref[pl.ds(r, 1), :]
        w = w_ref[pl.ds(r, 1), :]
        grow = jnp.exp(d * steps)
        shrink = w * jnp.exp(-d * steps)
        after = w * jnp.exp(-d * (steps + 1.0))
        tail = jnp.exp(-d * float(CHUNK - 1))
        hop = jnp.exp(-d * float(CHUNK))
        state = jnp.zeros((1, width), jnp.float32)
        for k in range(chunks):
            rows = slice(k * CHUNK, (k + 1) * CHUNK)
            scaled = grow * g_ref[rows, :]
            high = scaled.astype(jnp.bfloat16)
            low = (scaled - high.astype(jnp.float32)).astype(jnp.bfloat16)
            y = jnp.dot(lower, high, preferred_element_type=jnp.float32) + jnp.dot(
                lower, low, preferred_element_type=jnp.float32
            )
            out_ref[rows, :] += shrink * y + after * state
            state = hop * state + tail * y[CHUNK - 1 : CHUNK, :]
        total_ref[pl.ds(r, 1), :] = state
        return carry

    lax.fori_loop(0, d_ref.shape[0], mode, 0)


def modal_conv(gated, residues, decays):
    span, width = gated.shape
    half = span // 2
    groups = lax.axis_size("u")
    weight = residues * jnp.sqrt(-jnp.expm1(-2.0 * decays))
    g = gated.astype(jnp.float32)
    packed = jnp.concatenate([g[:half], g[half:]], axis=1)
    decays2 = jnp.concatenate([decays, decays], axis=1)
    weight2 = jnp.concatenate([weight, weight], axis=1)
    local, ends = pl.pallas_call(
        conv_kernel,
        out_shape=(
            jax.ShapeDtypeStruct((half, 2 * width), jnp.float32),
            jax.ShapeDtypeStruct(decays2.shape, jnp.float32),
        ),
        interpret=INTERPRET,
    )(packed, decays2, weight2)
    hop_half = jnp.exp(-decays * float(half))
    first_end, second_end = ends[:, :width], ends[:, width:]
    total = hop_half * first_end + second_end
    outer = None
    for m in range(1, groups):
        term = from_behind(total, "u", m)
        if m > 1:
            term = jnp.exp(-decays * float(span * (m - 1))) * term
        outer = term if outer is None else outer + term
    if outer is None:
        entry = jnp.concatenate([jnp.zeros_like(first_end), first_end], axis=1)
    else:
        entry = jnp.concatenate([outer, hop_half * outer + first_end], axis=1)
    steps = jnp.arange(half, dtype=jnp.float32)
    after = jnp.exp(-decays2[:, None, :] * (steps[None, :, None] + 1.0))
    joined = local + jnp.sum((weight2 * entry)[:, None, :] * after, axis=0)
    return jnp.concatenate([joined[:, :width], joined[:, width:]], axis=0)


def shards(
    query_input, key_input, value_input, short_filter, residues, decays, skip_gain, head_weight
):
    tokens, chan_width = query_input.shape
    width_u = lax.axis_size("u")
    width_v = lax.axis_size("v")
    piece = head_weight.shape[1]
    span = tokens * width_v
    narrow = width_u * piece
    before = from_behind(
        jnp.stack([query_input[-2:], key_input[-2:], value_input[-2:]], axis=0), ("u", "v"), 1
    )
    key_short = short_pass(key_input, before[1], short_filter[:, 1])
    value_short = short_pass(value_input, before[2], short_filter[:, 2])
    gated_rows = (key_short * value_short).astype(jnp.bfloat16)
    def by_target(values):
        depth = values.shape[0]
        shaped = values.reshape(depth, width_u, width_v, piece)
        return jnp.transpose(shaped, (2, 0, 1, 3)).reshape(width_v, depth, narrow)

    payload = jnp.concatenate(
        [by_target(before[0]), by_target(query_input), by_target(gated_rows)], axis=1
    )
    depth = payload.shape[1]
    columns = lax.all_to_all(payload, "v", split_axis=0, concat_axis=0, tiled=True)
    query_before = columns[0, :2]
    query_cols = columns[:, 2 : 2 + tokens].reshape(span, narrow)
    gated = columns[:, 2 + tokens :].reshape(span, narrow)
    head_weight, gated = lax.optimization_barrier((head_weight, gated))
    weight_rep = jnp.broadcast_to(head_weight[None], (width_u,) + head_weight.shape)
    weight_cols = lax.all_to_all(weight_rep, "u", split_axis=0, concat_axis=0, tiled=True)
    weight_cols = jnp.transpose(weight_cols, (1, 0, 2, 3)).reshape(
        head_weight.shape[0], narrow, head_weight.shape[2]
    )
    sf = short_filter.reshape(3, 3, width_u, width_v, piece)
    sf = jnp.transpose(sf, (0, 1, 3, 2, 4))
    sf = lax.dynamic_index_in_dim(sf, lax.axis_index("v"), axis=2, keepdims=False)
    sf = sf.reshape(3, 3, narrow)

    def pick(values):
        shaped = values.reshape(values.shape[0], width_u, width_v, piece)
        shaped = lax.dynamic_index_in_dim(shaped, lax.axis_index("v"), axis=2, keepdims=False)
        return shaped.reshape(values.shape[0], narrow)

    query_short = short_pass(query_cols, query_before, sf[:, 0])
    convolved = modal_conv(gated, pick(residues), pick(decays))
    gain = pick(skip_gain[None])[0]
    carried = (convolved + gain * gated.astype(jnp.float32)).astype(jnp.bfloat16)
    op_cols = (query_short * carried.astype(jnp.float32)).astype(jnp.bfloat16)
    rim_rows = from_behind(op_cols[:STRIDE], "u", -1)
    extended = jnp.concatenate([op_cols, rim_rows], axis=0)
    rows = span // STRIDE
    early_rows = extended[:span].reshape(rows, STRIDE, narrow)
    late_rows = extended[STRIDE:].reshape(rows, STRIDE, narrow)
    running = jnp.einsum(
        "jic,ico->jo", early_rows, weight_cols[:STRIDE], preferred_element_type=jnp.float32
    )
    partial_sum = running + jnp.einsum(
        "jic,ico->jo", late_rows, weight_cols[STRIDE:], preferred_element_type=jnp.float32
    )
    sums = partial_sum.astype(jnp.bfloat16).reshape(width_v, -1, width_u, 1, piece)
    extra = sums.shape[1]
    outgoing = jnp.concatenate(
        [op_cols.reshape(width_v, tokens, width_u, 1, piece), sums], axis=1
    )
    incoming = lax.all_to_all(outgoing, "v", split_axis=0, concat_axis=3, tiled=True)[0]
    operator_out = incoming[:tokens].reshape(tokens, chan_width)
    sums = jnp.transpose(incoming[tokens:], (2, 0, 1, 3)).astype(jnp.float32)
    block_sum = jnp.sum(sums.reshape(width_v, rows // width_v, -1), axis=0)
    probe_out = lax.psum_scatter(block_sum, "tp", scatter_dimension=0, tiled=True).astype(
        jnp.bfloat16
    )
    return (operator_out, probe_out)


def solution(mesh):
    seq_size, tp_size = mesh.devices.shape
    width_u = 4 if seq_size % 4 == 0 else 1
    split = jax.sharding.Mesh(
        mesh.devices.reshape(width_u, seq_size // width_u, tp_size), ("u", "v", "tp")
    )
    seq = ("u", "v")
    placed = (
        P(seq, "tp"),
        P(seq, "tp"),
        P(seq, "tp"),
        P(None, None, "tp"),
        P(None, "tp"),
        P(None, "tp"),
        P("tp"),
        P(None, ("tp", "u", "v"), None),
    )
    return jax.shard_map(
        shards,
        mesh=split,
        in_specs=placed,
        out_specs=(P(seq, "tp"), P(("u", "v", "tp"), None)),
        check_vma=False,
    )
```

```python
import jax
import jax.numpy as jnp
from jax import lax
from jax.experimental import pallas as pl
from jax.sharding import PartitionSpec as P

STRIDE = 16
CHUNK = 128
INTERPRET = False

highest = lax.Precision.HIGHEST


def from_behind(block, axis, distance):
    devices = range(lax.axis_size(axis))
    route = [(i - distance, i) for i in devices if i - distance in devices]
    return lax.ppermute(block, axis, route)


def short_pass(rows, before, tap_weights):
    joined = jnp.concatenate([before, rows], axis=0).astype(jnp.float32)
    row_count = rows.shape[0]
    return (
        tap_weights[0] * joined[2 : 2 + row_count]
        + tap_weights[1] * joined[1 : 1 + row_count]
        + tap_weights[2] * joined[0:row_count]
    )


def conv_kernel(g_ref, d_ref, w_ref, out_ref, total_ref):
    span, width = g_ref.shape
    chunks = span // CHUNK
    row = lax.broadcasted_iota(jnp.int32, (CHUNK, CHUNK), 0)
    col = lax.broadcasted_iota(jnp.int32, (CHUNK, CHUNK), 1)
    lower = (row >= col).astype(jnp.bfloat16)
    steps = lax.broadcasted_iota(jnp.int32, (CHUNK, width), 0).astype(jnp.float32)
    out_ref[...] = jnp.zeros(out_ref.shape, jnp.float32)

    def mode(r, carry):
        d = d_ref[pl.ds(r, 1), :]
        w = w_ref[pl.ds(r, 1), :]
        grow = jnp.exp(d * steps)
        shrink = w * jnp.exp(-d * steps)
        after = w * jnp.exp(-d * (steps + 1.0))
        tail = jnp.exp(-d * float(CHUNK - 1))
        hop = jnp.exp(-d * float(CHUNK))
        state = jnp.zeros((1, width), jnp.float32)
        for k in range(chunks):
            rows = slice(k * CHUNK, (k + 1) * CHUNK)
            scaled = grow * g_ref[rows, :]
            high = scaled.astype(jnp.bfloat16)
            low = (scaled - high.astype(jnp.float32)).astype(jnp.bfloat16)
            y = jnp.dot(lower, high, preferred_element_type=jnp.float32) + jnp.dot(
                lower, low, preferred_element_type=jnp.float32
            )
            out_ref[rows, :] += shrink * y + after * state
            state = hop * state + tail * y[CHUNK - 1 : CHUNK, :]
        total_ref[pl.ds(r, 1), :] = state
        return carry

    lax.fori_loop(0, d_ref.shape[0], mode, 0)


def modal_conv(gated, residues, decays):
    span, width = gated.shape
    half = span // 2
    groups = lax.axis_size("u")
    weight = residues * jnp.sqrt(-jnp.expm1(-2.0 * decays))
    g = gated.astype(jnp.float32)
    packed = jnp.concatenate([g[:half], g[half:]], axis=1)
    decays2 = jnp.concatenate([decays, decays], axis=1)
    weight2 = jnp.concatenate([weight, weight], axis=1)
    local, ends = pl.pallas_call(
        conv_kernel,
        out_shape=(
            jax.ShapeDtypeStruct((half, 2 * width), jnp.float32),
            jax.ShapeDtypeStruct(decays2.shape, jnp.float32),
        ),
        interpret=INTERPRET,
    )(packed, decays2, weight2)
    hop_half = jnp.exp(-decays * float(half))
    first_end, second_end = ends[:, :width], ends[:, width:]
    total = hop_half * first_end + second_end
    outer = None
    if groups > 1:
        shared = jnp.broadcast_to(total[None], (groups,) + total.shape)
        shared = lax.all_to_all(shared, "u", split_axis=0, concat_axis=0, tiled=True)
        source = jnp.arange(groups, dtype=jnp.int32)
        lag = lax.axis_index("u") - 1 - source
        gap = (float(span) * jnp.maximum(lag, 0).astype(jnp.float32))[:, None, None]
        factor = jnp.where((lag >= 0)[:, None, None], jnp.exp(-decays[None] * gap), 0.0)
        outer = jnp.sum(factor * shared, axis=0)
    if outer is None:
        entry = jnp.concatenate([jnp.zeros_like(first_end), first_end], axis=1)
    else:
        entry = jnp.concatenate([outer, hop_half * outer + first_end], axis=1)
    steps = jnp.arange(half, dtype=jnp.float32)
    after = jnp.exp(-decays2[:, None, :] * (steps[None, :, None] + 1.0))
    joined = local + jnp.sum((weight2 * entry)[:, None, :] * after, axis=0)
    return jnp.concatenate([joined[:, :width], joined[:, width:]], axis=0)


def shards(
    query_input, key_input, value_input, short_filter, residues, decays, skip_gain, head_weight
):
    tokens, chan_width = query_input.shape
    width_u = lax.axis_size("u")
    width_v = lax.axis_size("v")
    piece = head_weight.shape[1]
    span = tokens * width_v
    narrow = width_u * piece
    before = from_behind(
        jnp.stack([query_input[-2:], key_input[-2:], value_input[-2:]], axis=0), ("u", "v"), 1
    )
    key_short = short_pass(key_input, before[1], short_filter[:, 1])
    value_short = short_pass(value_input, before[2], short_filter[:, 2])
    gated_rows = (key_short * value_short).astype(jnp.bfloat16)
    def by_target(values):
        depth = values.shape[0]
        shaped = values.reshape(depth, width_u, width_v, piece)
        return jnp.transpose(shaped, (2, 0, 1, 3)).reshape(width_v, depth, narrow)

    payload = jnp.concatenate(
        [by_target(before[0]), by_target(query_input), by_target(gated_rows)], axis=1
    )
    depth = payload.shape[1]
    columns = lax.all_to_all(payload, "v", split_axis=0, concat_axis=0, tiled=True)
    query_before = columns[0, :2]
    query_cols = columns[:, 2 : 2 + tokens].reshape(span, narrow)
    gated = columns[:, 2 + tokens :].reshape(span, narrow)
    head_weight, gated = lax.optimization_barrier((head_weight, gated))
    weight_rep = jnp.broadcast_to(head_weight[None], (width_u,) + head_weight.shape)
    weight_cols = lax.all_to_all(weight_rep, "u", split_axis=0, concat_axis=0, tiled=True)
    weight_cols = jnp.transpose(weight_cols, (1, 0, 2, 3)).reshape(
        head_weight.shape[0], narrow, head_weight.shape[2]
    )
    sf = short_filter.reshape(3, 3, width_u, width_v, piece)
    sf = jnp.transpose(sf, (0, 1, 3, 2, 4))
    sf = lax.dynamic_index_in_dim(sf, lax.axis_index("v"), axis=2, keepdims=False)
    sf = sf.reshape(3, 3, narrow)

    def pick(values):
        shaped = values.reshape(values.shape[0], width_u, width_v, piece)
        shaped = lax.dynamic_index_in_dim(shaped, lax.axis_index("v"), axis=2, keepdims=False)
        return shaped.reshape(values.shape[0], narrow)

    query_short = short_pass(query_cols, query_before, sf[:, 0])
    convolved = modal_conv(gated, pick(residues), pick(decays))
    gain = pick(skip_gain[None])[0]
    carried = (convolved + gain * gated.astype(jnp.float32)).astype(jnp.bfloat16)
    op_cols = (query_short * carried.astype(jnp.float32)).astype(jnp.bfloat16)
    rim_rows = from_behind(op_cols[:STRIDE], "u", -1)
    extended = jnp.concatenate([op_cols, rim_rows], axis=0)
    rows = span // STRIDE
    early_rows = extended[:span].reshape(rows, STRIDE, narrow)
    late_rows = extended[STRIDE:].reshape(rows, STRIDE, narrow)
    running = jnp.einsum(
        "jic,ico->jo", early_rows, weight_cols[:STRIDE], preferred_element_type=jnp.float32
    )
    partial_sum = running + jnp.einsum(
        "jic,ico->jo", late_rows, weight_cols[STRIDE:], preferred_element_type=jnp.float32
    )
    sums = partial_sum.astype(jnp.bfloat16).reshape(width_v, -1, width_u, 1, piece)
    extra = sums.shape[1]
    outgoing = jnp.concatenate(
        [op_cols.reshape(width_v, tokens, width_u, 1, piece), sums], axis=1
    )
    incoming = lax.all_to_all(outgoing, "v", split_axis=0, concat_axis=3, tiled=True)[0]
    operator_out = incoming[:tokens].reshape(tokens, chan_width)
    sums = jnp.transpose(incoming[tokens:], (2, 0, 1, 3)).astype(jnp.float32)
    block_sum = jnp.sum(sums.reshape(width_v, rows // width_v, -1), axis=0)
    probe_out = lax.psum_scatter(block_sum, "tp", scatter_dimension=0, tiled=True).astype(
        jnp.bfloat16
    )
    return (operator_out, probe_out)


def solution(mesh):
    seq_size, tp_size = mesh.devices.shape
    width_u = 4 if seq_size % 4 == 0 else 1
    split = jax.sharding.Mesh(
        mesh.devices.reshape(width_u, seq_size // width_u, tp_size), ("u", "v", "tp")
    )
    seq = ("u", "v")
    placed = (
        P(seq, "tp"),
        P(seq, "tp"),
        P(seq, "tp"),
        P(None, None, "tp"),
        P(None, "tp"),
        P(None, "tp"),
        P("tp"),
        P(None, ("tp", "u", "v"), None),
    )
    return jax.shard_map(
        shards,
        mesh=split,
        in_specs=placed,
        out_specs=(P(seq, "tp"), P(("u", "v", "tp"), None)),
        check_vma=False,
    )
```

```python
import jax
import jax.numpy as jnp
from jax import lax
from jax.experimental import pallas as pl
from jax.sharding import PartitionSpec as P

STRIDE = 16
CHUNK = 128
INTERPRET = False

highest = lax.Precision.HIGHEST


def from_behind(block, axis, distance):
    devices = range(lax.axis_size(axis))
    route = [(i - distance, i) for i in devices if i - distance in devices]
    return lax.ppermute(block, axis, route)


def short_pass(rows, before, tap_weights):
    joined = jnp.concatenate([before, rows], axis=0).astype(jnp.float32)
    row_count = rows.shape[0]
    return (
        tap_weights[0] * joined[2 : 2 + row_count]
        + tap_weights[1] * joined[1 : 1 + row_count]
        + tap_weights[2] * joined[0:row_count]
    )


def conv_kernel(g_ref, d_ref, w_ref, out_ref, total_ref):
    span, width = g_ref.shape
    chunks = span // CHUNK
    row = lax.broadcasted_iota(jnp.int32, (CHUNK, CHUNK), 0)
    col = lax.broadcasted_iota(jnp.int32, (CHUNK, CHUNK), 1)
    lower = (row >= col).astype(jnp.bfloat16)
    steps = lax.broadcasted_iota(jnp.int32, (CHUNK, width), 0).astype(jnp.float32)
    out_ref[...] = jnp.zeros(out_ref.shape, jnp.float32)

    def mode(r, carry):
        d = d_ref[pl.ds(r, 1), :]
        w = w_ref[pl.ds(r, 1), :]
        grow = jnp.exp(d * steps)
        shrink = w * jnp.exp(-d * steps)
        after = w * jnp.exp(-d * (steps + 1.0))
        tail = jnp.exp(-d * float(CHUNK - 1))
        hop = jnp.exp(-d * float(CHUNK))
        state = jnp.zeros((1, width), jnp.float32)
        for k in range(chunks):
            rows = slice(k * CHUNK, (k + 1) * CHUNK)
            scaled = grow * g_ref[rows, :]
            high = scaled.astype(jnp.bfloat16)
            low = (scaled - high.astype(jnp.float32)).astype(jnp.bfloat16)
            y = jnp.dot(lower, high, preferred_element_type=jnp.float32) + jnp.dot(
                lower, low, preferred_element_type=jnp.float32
            )
            out_ref[rows, :] += shrink * y + after * state
            state = hop * state + tail * y[CHUNK - 1 : CHUNK, :]
        total_ref[pl.ds(r, 1), :] = state
        return carry

    lax.fori_loop(0, d_ref.shape[0], mode, 0)


def modal_conv(gated, residues, decays):
    span, width = gated.shape
    half = span // 2
    groups = lax.axis_size("u")
    weight = residues * jnp.sqrt(-jnp.expm1(-2.0 * decays))
    g = gated.astype(jnp.float32)
    packed = jnp.concatenate([g[:half], g[half:]], axis=1)
    decays2 = jnp.concatenate([decays, decays], axis=1)
    weight2 = jnp.concatenate([weight, weight], axis=1)
    local, ends = pl.pallas_call(
        conv_kernel,
        out_shape=(
            jax.ShapeDtypeStruct((half, 2 * width), jnp.float32),
            jax.ShapeDtypeStruct(decays2.shape, jnp.float32),
        ),
        interpret=INTERPRET,
    )(packed, decays2, weight2)
    hop_half = jnp.exp(-decays * float(half))
    first_end, second_end = ends[:, :width], ends[:, width:]
    total = hop_half * first_end + second_end
    outer = None
    if groups > 1:
        shared = jnp.broadcast_to(total[None], (groups,) + total.shape)
        shared = lax.all_to_all(shared, "u", split_axis=0, concat_axis=0, tiled=True)
        source = jnp.arange(groups, dtype=jnp.int32)
        lag = lax.axis_index("u") - 1 - source
        gap = (float(span) * jnp.maximum(lag, 0).astype(jnp.float32))[:, None, None]
        factor = jnp.where((lag >= 0)[:, None, None], jnp.exp(-decays[None] * gap), 0.0)
        outer = jnp.sum(factor * shared, axis=0)
    if outer is None:
        entry = jnp.concatenate([jnp.zeros_like(first_end), first_end], axis=1)
    else:
        entry = jnp.concatenate([outer, hop_half * outer + first_end], axis=1)
    steps = jnp.arange(half, dtype=jnp.float32)
    after = jnp.exp(-decays2[:, None, :] * (steps[None, :, None] + 1.0))
    joined = local + jnp.sum((weight2 * entry)[:, None, :] * after, axis=0)
    return jnp.concatenate([joined[:, :width], joined[:, width:]], axis=0)


def shards(
    query_input, key_input, value_input, short_filter, residues, decays, skip_gain, head_weight
):
    tokens, chan_width = query_input.shape
    width_u = lax.axis_size("u")
    width_v = lax.axis_size("v")
    piece = head_weight.shape[1]
    span = tokens * width_v
    narrow = width_u * piece
    before = from_behind(
        jnp.stack([query_input[-2:], key_input[-2:], value_input[-2:]], axis=0), ("u", "v"), 1
    )
    key_short = short_pass(key_input, before[1], short_filter[:, 1])
    value_short = short_pass(value_input, before[2], short_filter[:, 2])
    gated_rows = (key_short * value_short).astype(jnp.bfloat16)
    def by_target(values):
        depth = values.shape[0]
        shaped = values.reshape(depth, width_u, width_v, piece)
        return jnp.transpose(shaped, (2, 0, 1, 3)).reshape(width_v, depth, narrow)

    payload = jnp.concatenate(
        [by_target(before[0]), by_target(query_input), by_target(gated_rows)], axis=1
    )
    depth = payload.shape[1]
    columns = lax.all_to_all(payload, "v", split_axis=0, concat_axis=0, tiled=True)
    query_before = columns[0, :2]
    query_cols = columns[:, 2 : 2 + tokens].reshape(span, narrow)
    gated = columns[:, 2 + tokens :].reshape(span, narrow)
    head_weight, gated = lax.optimization_barrier((head_weight, gated))
    weight_rep = jnp.broadcast_to(head_weight[None], (width_u,) + head_weight.shape)
    weight_cols = lax.all_to_all(weight_rep, "u", split_axis=0, concat_axis=0, tiled=True)
    weight_cols = jnp.transpose(weight_cols, (1, 0, 2, 3)).reshape(
        head_weight.shape[0], narrow, head_weight.shape[2]
    )
    sf = short_filter.reshape(3, 3, width_u, width_v, piece)
    sf = jnp.transpose(sf, (0, 1, 3, 2, 4))
    sf = lax.dynamic_index_in_dim(sf, lax.axis_index("v"), axis=2, keepdims=False)
    sf = sf.reshape(3, 3, narrow)

    def pick(values):
        shaped = values.reshape(values.shape[0], width_u, width_v, piece)
        shaped = lax.dynamic_index_in_dim(shaped, lax.axis_index("v"), axis=2, keepdims=False)
        return shaped.reshape(values.shape[0], narrow)

    query_short = short_pass(query_cols, query_before, sf[:, 0])
    convolved = modal_conv(gated, pick(residues), pick(decays))
    gain = pick(skip_gain[None])[0]
    carried = (convolved + gain * gated.astype(jnp.float32)).astype(jnp.bfloat16)
    op_cols = (query_short * carried.astype(jnp.float32)).astype(jnp.bfloat16)
    rim_rows = from_behind(op_cols[:STRIDE], "u", -1)
    extended = jnp.concatenate([op_cols, rim_rows], axis=0)
    rows = span // STRIDE
    early_rows = extended[:span].reshape(rows, STRIDE, narrow)
    late_rows = extended[STRIDE:].reshape(rows, STRIDE, narrow)
    running = jnp.einsum(
        "jic,ico->jo", early_rows, weight_cols[:STRIDE], preferred_element_type=jnp.float32
    )
    partial_sum = running + jnp.einsum(
        "jic,ico->jo", late_rows, weight_cols[STRIDE:], preferred_element_type=jnp.float32
    )
    sums = partial_sum.astype(jnp.bfloat16).reshape(width_v, -1, width_u, 1, piece)
    extra = sums.shape[1]
    outgoing = jnp.concatenate(
        [op_cols.reshape(width_v, tokens, width_u, 1, piece), sums], axis=1
    )
    incoming = lax.all_to_all(outgoing, "v", split_axis=0, concat_axis=3, tiled=True)[0]
    operator_out = incoming[:tokens].reshape(tokens, chan_width)
    sums = jnp.transpose(incoming[tokens:], (2, 0, 1, 3)).astype(jnp.float32)
    block_sum = jnp.sum(sums.reshape(width_v, rows // width_v, -1), axis=0)
    probe_out = lax.psum_scatter(block_sum, "tp", scatter_dimension=0, tiled=True).astype(
        jnp.bfloat16
    )
    return (operator_out, probe_out)


def solution(mesh):
    seq_size, tp_size = mesh.devices.shape
    width_u = 8 if seq_size % 8 == 0 else 1
    split = jax.sharding.Mesh(
        mesh.devices.reshape(width_u, seq_size // width_u, tp_size), ("u", "v", "tp")
    )
    seq = ("u", "v")
    placed = (
        P(seq, "tp"),
        P(seq, "tp"),
        P(seq, "tp"),
        P(None, None, "tp"),
        P(None, "tp"),
        P(None, "tp"),
        P("tp"),
        P(None, ("tp", "u", "v"), None),
    )
    return jax.shard_map(
        shards,
        mesh=split,
        in_specs=placed,
        out_specs=(P(seq, "tp"), P(("u", "v", "tp"), None)),
        check_vma=False,
    )
```

```python
import jax
import jax.numpy as jnp
from jax import lax
from jax.experimental import pallas as pl
from jax.sharding import PartitionSpec as P

STRIDE = 16
CHUNK = 128
INTERPRET = False

highest = lax.Precision.HIGHEST


def from_behind(block, axis, distance):
    devices = range(lax.axis_size(axis))
    route = [(i - distance, i) for i in devices if i - distance in devices]
    return lax.ppermute(block, axis, route)


def short_pass(rows, before, tap_weights):
    joined = jnp.concatenate([before, rows], axis=0).astype(jnp.float32)
    row_count = rows.shape[0]
    return (
        tap_weights[0] * joined[2 : 2 + row_count]
        + tap_weights[1] * joined[1 : 1 + row_count]
        + tap_weights[2] * joined[0:row_count]
    )


def conv_kernel(g_ref, d_ref, w_ref, out_ref, total_ref):
    span, width = g_ref.shape
    chunks = span // CHUNK
    row = lax.broadcasted_iota(jnp.int32, (CHUNK, CHUNK), 0)
    col = lax.broadcasted_iota(jnp.int32, (CHUNK, CHUNK), 1)
    lower = (row >= col).astype(jnp.bfloat16)
    steps = lax.broadcasted_iota(jnp.int32, (CHUNK, width), 0).astype(jnp.float32)
    out_ref[...] = jnp.zeros(out_ref.shape, jnp.float32)

    def mode(r, carry):
        d = d_ref[pl.ds(r, 1), :]
        w = w_ref[pl.ds(r, 1), :]
        grow = jnp.exp(d * steps)
        shrink = w * jnp.exp(-d * steps)
        after = w * jnp.exp(-d * (steps + 1.0))
        tail = jnp.exp(-d * float(CHUNK - 1))
        hop = jnp.exp(-d * float(CHUNK))
        state = jnp.zeros((1, width), jnp.float32)
        for k in range(chunks):
            rows = slice(k * CHUNK, (k + 1) * CHUNK)
            scaled = grow * g_ref[rows, :]
            high = scaled.astype(jnp.bfloat16)
            low = (scaled - high.astype(jnp.float32)).astype(jnp.bfloat16)
            y = jnp.dot(lower, high, preferred_element_type=jnp.float32) + jnp.dot(
                lower, low, preferred_element_type=jnp.float32
            )
            out_ref[rows, :] += shrink * y + after * state
            state = hop * state + tail * y[CHUNK - 1 : CHUNK, :]
        total_ref[pl.ds(r, 1), :] = state
        return carry

    lax.fori_loop(0, d_ref.shape[0], mode, 0)


def modal_conv(gated, residues, decays):
    span, width = gated.shape
    half = span // 2
    groups = lax.axis_size("u")
    weight = residues * jnp.sqrt(-jnp.expm1(-2.0 * decays))
    g = gated.astype(jnp.float32)
    packed = jnp.concatenate([g[:half], g[half:]], axis=1)
    decays2 = jnp.concatenate([decays, decays], axis=1)
    weight2 = jnp.concatenate([weight, weight], axis=1)
    local, ends = pl.pallas_call(
        conv_kernel,
        out_shape=(
            jax.ShapeDtypeStruct((half, 2 * width), jnp.float32),
            jax.ShapeDtypeStruct(decays2.shape, jnp.float32),
        ),
        interpret=INTERPRET,
    )(packed, decays2, weight2)
    hop_half = jnp.exp(-decays * float(half))
    first_end, second_end = ends[:, :width], ends[:, width:]
    total = hop_half * first_end + second_end
    outer = None
    if groups > 1:
        shared = jnp.broadcast_to(total[None], (groups,) + total.shape)
        shared = lax.all_to_all(shared, "u", split_axis=0, concat_axis=0, tiled=True)
        source = jnp.arange(groups, dtype=jnp.int32)
        lag = lax.axis_index("u") - 1 - source
        gap = (float(span) * jnp.maximum(lag, 0).astype(jnp.float32))[:, None, None]
        factor = jnp.where((lag >= 0)[:, None, None], jnp.exp(-decays[None] * gap), 0.0)
        outer = jnp.sum(factor * shared, axis=0)
    if outer is None:
        entry = jnp.concatenate([jnp.zeros_like(first_end), first_end], axis=1)
    else:
        entry = jnp.concatenate([outer, hop_half * outer + first_end], axis=1)
    steps = jnp.arange(half, dtype=jnp.float32)
    after = jnp.exp(-decays2[:, None, :] * (steps[None, :, None] + 1.0))
    joined = local + jnp.sum((weight2 * entry)[:, None, :] * after, axis=0)
    return jnp.concatenate([joined[:, :width], joined[:, width:]], axis=0)


def shards(
    query_input, key_input, value_input, short_filter, residues, decays, skip_gain, head_weight
):
    tokens, chan_width = query_input.shape
    width_u = lax.axis_size("u")
    width_v = lax.axis_size("v")
    piece = head_weight.shape[1]
    span = tokens * width_v
    narrow = width_u * piece
    before = from_behind(
        jnp.stack([query_input[-2:], key_input[-2:], value_input[-2:]], axis=0), ("u", "v"), 1
    )
    key_short = short_pass(key_input, before[1], short_filter[:, 1])
    value_short = short_pass(value_input, before[2], short_filter[:, 2])
    gated_rows = (key_short * value_short).astype(jnp.bfloat16)
    def by_target(values):
        depth = values.shape[0]
        shaped = values.reshape(depth, width_u, width_v, piece)
        return jnp.transpose(shaped, (2, 0, 1, 3)).reshape(width_v, depth, narrow)

    payload = jnp.concatenate(
        [by_target(before[0]), by_target(query_input), by_target(gated_rows)], axis=1
    )
    depth = payload.shape[1]
    columns = lax.all_to_all(payload, "v", split_axis=0, concat_axis=0, tiled=True)
    query_before = columns[0, :2]
    query_cols = columns[:, 2 : 2 + tokens].reshape(span, narrow)
    gated = columns[:, 2 + tokens :].reshape(span, narrow)
    head_weight, gated = lax.optimization_barrier((head_weight, gated))
    weight_cols = lax.all_gather(head_weight, "u", axis=1, tiled=True)
    sf = short_filter.reshape(3, 3, width_u, width_v, piece)
    sf = jnp.transpose(sf, (0, 1, 3, 2, 4))
    sf = lax.dynamic_index_in_dim(sf, lax.axis_index("v"), axis=2, keepdims=False)
    sf = sf.reshape(3, 3, narrow)

    def pick(values):
        shaped = values.reshape(values.shape[0], width_u, width_v, piece)
        shaped = lax.dynamic_index_in_dim(shaped, lax.axis_index("v"), axis=2, keepdims=False)
        return shaped.reshape(values.shape[0], narrow)

    query_short = short_pass(query_cols, query_before, sf[:, 0])
    convolved = modal_conv(gated, pick(residues), pick(decays))
    gain = pick(skip_gain[None])[0]
    carried = (convolved + gain * gated.astype(jnp.float32)).astype(jnp.bfloat16)
    op_cols = (query_short * carried.astype(jnp.float32)).astype(jnp.bfloat16)
    rim_rows = from_behind(op_cols[:STRIDE], "u", -1)
    extended = jnp.concatenate([op_cols, rim_rows], axis=0)
    rows = span // STRIDE
    early_rows = extended[:span].reshape(rows, STRIDE, narrow)
    late_rows = extended[STRIDE:].reshape(rows, STRIDE, narrow)
    running = jnp.einsum(
        "jic,ico->jo", early_rows, weight_cols[:STRIDE], preferred_element_type=jnp.float32
    )
    partial_sum = running + jnp.einsum(
        "jic,ico->jo", late_rows, weight_cols[STRIDE:], preferred_element_type=jnp.float32
    )
    sums = partial_sum.astype(jnp.bfloat16).reshape(width_v, -1, width_u, 1, piece)
    extra = sums.shape[1]
    outgoing = jnp.concatenate(
        [op_cols.reshape(width_v, tokens, width_u, 1, piece), sums], axis=1
    )
    incoming = lax.all_to_all(outgoing, "v", split_axis=0, concat_axis=3, tiled=True)[0]
    operator_out = incoming[:tokens].reshape(tokens, chan_width)
    sums = jnp.transpose(incoming[tokens:], (2, 0, 1, 3)).astype(jnp.float32)
    block_sum = jnp.sum(sums.reshape(width_v, rows // width_v, -1), axis=0)
    probe_out = lax.psum_scatter(block_sum, "tp", scatter_dimension=0, tiled=True).astype(
        jnp.bfloat16
    )
    return (operator_out, probe_out)


def solution(mesh):
    seq_size, tp_size = mesh.devices.shape
    width_u = 8 if seq_size % 8 == 0 else 1
    split = jax.sharding.Mesh(
        mesh.devices.reshape(width_u, seq_size // width_u, tp_size), ("u", "v", "tp")
    )
    seq = ("u", "v")
    placed = (
        P(seq, "tp"),
        P(seq, "tp"),
        P(seq, "tp"),
        P(None, None, "tp"),
        P(None, "tp"),
        P(None, "tp"),
        P("tp"),
        P(None, ("tp", "u", "v"), None),
    )
    return jax.shard_map(
        shards,
        mesh=split,
        in_specs=placed,
        out_specs=(P(seq, "tp"), P(("u", "v", "tp"), None)),
        check_vma=False,
    )
```

```python
import jax
import jax.numpy as jnp
from jax import lax
from jax.experimental import pallas as pl
from jax.sharding import PartitionSpec as P

STRIDE = 16
CHUNK = 128
INTERPRET = False

highest = lax.Precision.HIGHEST


def from_behind(block, axis, distance):
    devices = range(lax.axis_size(axis))
    route = [(i - distance, i) for i in devices if i - distance in devices]
    return lax.ppermute(block, axis, route)


def short_pass(rows, before, tap_weights):
    joined = jnp.concatenate([before, rows], axis=0).astype(jnp.float32)
    row_count = rows.shape[0]
    return (
        tap_weights[0] * joined[2 : 2 + row_count]
        + tap_weights[1] * joined[1 : 1 + row_count]
        + tap_weights[2] * joined[0:row_count]
    )


def conv_kernel(g_ref, d_ref, w_ref, out_ref, total_ref):
    span, width = g_ref.shape
    chunks = span // CHUNK
    row = lax.broadcasted_iota(jnp.int32, (CHUNK, CHUNK), 0)
    col = lax.broadcasted_iota(jnp.int32, (CHUNK, CHUNK), 1)
    lower = (row >= col).astype(jnp.bfloat16)
    steps = lax.broadcasted_iota(jnp.int32, (CHUNK, width), 0).astype(jnp.float32)
    out_ref[...] = jnp.zeros(out_ref.shape, jnp.float32)

    def mode(r, carry):
        d = d_ref[pl.ds(r, 1), :]
        w = w_ref[pl.ds(r, 1), :]
        grow = jnp.exp(d * steps)
        shrink = w * jnp.exp(-d * steps)
        after = w * jnp.exp(-d * (steps + 1.0))
        tail = jnp.exp(-d * float(CHUNK - 1))
        hop = jnp.exp(-d * float(CHUNK))
        state = jnp.zeros((1, width), jnp.float32)
        for k in range(chunks):
            rows = slice(k * CHUNK, (k + 1) * CHUNK)
            scaled = grow * g_ref[rows, :]
            high = scaled.astype(jnp.bfloat16)
            low = (scaled - high.astype(jnp.float32)).astype(jnp.bfloat16)
            y = jnp.dot(lower, high, preferred_element_type=jnp.float32) + jnp.dot(
                lower, low, preferred_element_type=jnp.float32
            )
            out_ref[rows, :] += shrink * y + after * state
            state = hop * state + tail * y[CHUNK - 1 : CHUNK, :]
        total_ref[pl.ds(r, 1), :] = state
        return carry

    lax.fori_loop(0, d_ref.shape[0], mode, 0)


def modal_conv(gated, residues, decays):
    span, width = gated.shape
    parts = max(1, min(128 // width, span // CHUNK))
    seg = span // parts
    groups = lax.axis_size("u")
    weight = residues * jnp.sqrt(-jnp.expm1(-2.0 * decays))
    g = gated.astype(jnp.float32)
    packed = jnp.concatenate([g[s * seg : (s + 1) * seg] for s in range(parts)], axis=1)
    decays_p = jnp.concatenate([decays] * parts, axis=1)
    weight_p = jnp.concatenate([weight] * parts, axis=1)
    local, ends = pl.pallas_call(
        conv_kernel,
        out_shape=(
            jax.ShapeDtypeStruct((seg, parts * width), jnp.float32),
            jax.ShapeDtypeStruct(decays_p.shape, jnp.float32),
        ),
        interpret=INTERPRET,
    )(packed, decays_p, weight_p)
    ends = ends.reshape(decays.shape[0], parts, width)
    index = jnp.arange(parts)
    lag = index[:, None] - 1 - index[None, :]
    gap = (float(seg) * jnp.maximum(lag, 0).astype(jnp.float32))[None, :, :, None]
    table = jnp.where((lag >= 0)[None, :, :, None], jnp.exp(-decays[:, None, None, :] * gap), 0.0)
    inner = jnp.sum(table * ends[:, None, :, :], axis=2)
    last = (float(seg) * (parts - 1 - index).astype(jnp.float32))[None, :, None]
    total = jnp.sum(jnp.exp(-decays[:, None, :] * last) * ends, axis=1)
    outer = None
    for m in range(1, groups):
        term = from_behind(total, "u", m)
        if m > 1:
            term = jnp.exp(-decays * float(span * (m - 1))) * term
        outer = term if outer is None else outer + term
    if outer is not None:
        lead = (float(seg) * index.astype(jnp.float32))[None, :, None]
        inner = inner + jnp.exp(-decays[:, None, :] * lead) * outer[:, None, :]
    entry = inner.reshape(decays.shape[0], parts * width)
    steps = jnp.arange(seg, dtype=jnp.float32)
    after = jnp.exp(-decays_p[:, None, :] * (steps[None, :, None] + 1.0))
    joined = local + jnp.sum((weight_p * entry)[:, None, :] * after, axis=0)
    return jnp.concatenate([joined[:, s * width : (s + 1) * width] for s in range(parts)], axis=0)


def shards(
    query_input, key_input, value_input, short_filter, residues, decays, skip_gain, head_weight
):
    tokens, chan_width = query_input.shape
    width_u = lax.axis_size("u")
    width_v = lax.axis_size("v")
    piece = head_weight.shape[1]
    span = tokens * width_v
    narrow = width_u * piece
    before = from_behind(
        jnp.stack([query_input[-2:], key_input[-2:], value_input[-2:]], axis=0), ("u", "v"), 1
    )
    key_short = short_pass(key_input, before[1], short_filter[:, 1])
    value_short = short_pass(value_input, before[2], short_filter[:, 2])
    gated_rows = (key_short * value_short).astype(jnp.bfloat16)
    def by_target(values):
        depth = values.shape[0]
        shaped = values.reshape(depth, width_u, width_v, piece)
        return jnp.transpose(shaped, (2, 0, 1, 3)).reshape(width_v, depth, narrow)

    payload = jnp.concatenate(
        [by_target(before[0]), by_target(query_input), by_target(gated_rows)], axis=1
    )
    depth = payload.shape[1]
    columns = lax.all_to_all(payload, "v", split_axis=0, concat_axis=0, tiled=True)
    query_before = columns[0, :2]
    query_cols = columns[:, 2 : 2 + tokens].reshape(span, narrow)
    gated = columns[:, 2 + tokens :].reshape(span, narrow)
    head_weight, gated = lax.optimization_barrier((head_weight, gated))
    weight_rep = jnp.broadcast_to(head_weight[None], (width_u,) + head_weight.shape)
    weight_cols = lax.all_to_all(weight_rep, "u", split_axis=0, concat_axis=0, tiled=True)
    weight_cols = jnp.transpose(weight_cols, (1, 0, 2, 3)).reshape(
        head_weight.shape[0], narrow, head_weight.shape[2]
    )
    sf = short_filter.reshape(3, 3, width_u, width_v, piece)
    sf = jnp.transpose(sf, (0, 1, 3, 2, 4))
    sf = lax.dynamic_index_in_dim(sf, lax.axis_index("v"), axis=2, keepdims=False)
    sf = sf.reshape(3, 3, narrow)

    def pick(values):
        shaped = values.reshape(values.shape[0], width_u, width_v, piece)
        shaped = lax.dynamic_index_in_dim(shaped, lax.axis_index("v"), axis=2, keepdims=False)
        return shaped.reshape(values.shape[0], narrow)

    query_short = short_pass(query_cols, query_before, sf[:, 0])
    convolved = modal_conv(gated, pick(residues), pick(decays))
    gain = pick(skip_gain[None])[0]
    carried = (convolved + gain * gated.astype(jnp.float32)).astype(jnp.bfloat16)
    op_cols = (query_short * carried.astype(jnp.float32)).astype(jnp.bfloat16)
    if width_u > 1:
        rim_rows = from_behind(op_cols[:STRIDE], "u", -1)
    else:
        rim_rows = jnp.zeros_like(op_cols[:STRIDE])
    extended = jnp.concatenate([op_cols, rim_rows], axis=0)
    rows = span // STRIDE
    early_rows = extended[:span].reshape(rows, STRIDE, narrow)
    late_rows = extended[STRIDE:].reshape(rows, STRIDE, narrow)
    running = jnp.einsum(
        "jic,ico->jo", early_rows, weight_cols[:STRIDE], preferred_element_type=jnp.float32
    )
    partial_sum = running + jnp.einsum(
        "jic,ico->jo", late_rows, weight_cols[STRIDE:], preferred_element_type=jnp.float32
    )
    sums = partial_sum.astype(jnp.bfloat16).reshape(width_v, -1, width_u, 1, piece)
    extra = sums.shape[1]
    outgoing = jnp.concatenate(
        [op_cols.reshape(width_v, tokens, width_u, 1, piece), sums], axis=1
    )
    incoming = lax.all_to_all(outgoing, "v", split_axis=0, concat_axis=3, tiled=True)[0]
    operator_out = incoming[:tokens].reshape(tokens, chan_width)
    sums = jnp.transpose(incoming[tokens:], (2, 0, 1, 3)).astype(jnp.float32)
    block_sum = jnp.sum(sums.reshape(width_v, rows // width_v, -1), axis=0)
    probe_out = lax.psum_scatter(block_sum, "tp", scatter_dimension=0, tiled=True).astype(
        jnp.bfloat16
    )
    return (operator_out, probe_out)


def solution(mesh):
    seq_size, tp_size = mesh.devices.shape
    width_u = 1
    split = jax.sharding.Mesh(
        mesh.devices.reshape(width_u, seq_size // width_u, tp_size), ("u", "v", "tp")
    )
    seq = ("u", "v")
    placed = (
        P(seq, "tp"),
        P(seq, "tp"),
        P(seq, "tp"),
        P(None, None, "tp"),
        P(None, "tp"),
        P(None, "tp"),
        P("tp"),
        P(None, ("tp", "u", "v"), None),
    )
    return jax.shard_map(
        shards,
        mesh=split,
        in_specs=placed,
        out_specs=(P(seq, "tp"), P(("u", "v", "tp"), None)),
        check_vma=False,
    )
```

```python
import jax
import jax.numpy as jnp
from jax import lax
from jax.experimental import pallas as pl
from jax.sharding import PartitionSpec as P

STRIDE = 16
CHUNK = 128
INTERPRET = False

highest = lax.Precision.HIGHEST


def from_behind(block, axis, distance):
    devices = range(lax.axis_size(axis))
    route = [(i - distance, i) for i in devices if i - distance in devices]
    return lax.ppermute(block, axis, route)


def short_pass(rows, before, tap_weights):
    joined = jnp.concatenate([before, rows], axis=0).astype(jnp.float32)
    row_count = rows.shape[0]
    return (
        tap_weights[0] * joined[2 : 2 + row_count]
        + tap_weights[1] * joined[1 : 1 + row_count]
        + tap_weights[2] * joined[0:row_count]
    )


def conv_kernel(g_ref, d_ref, w_ref, out_ref, total_ref):
    span, width = g_ref.shape
    chunks = span // CHUNK
    row = lax.broadcasted_iota(jnp.int32, (CHUNK, CHUNK), 0)
    col = lax.broadcasted_iota(jnp.int32, (CHUNK, CHUNK), 1)
    lower = (row >= col).astype(jnp.bfloat16)
    steps = lax.broadcasted_iota(jnp.int32, (CHUNK, width), 0).astype(jnp.float32)
    out_ref[...] = jnp.zeros(out_ref.shape, jnp.float32)

    def mode(r, carry):
        d = d_ref[pl.ds(r, 1), :]
        w = w_ref[pl.ds(r, 1), :]
        grow = jnp.exp(d * steps)
        shrink = w * jnp.exp(-d * steps)
        after = w * jnp.exp(-d * (steps + 1.0))
        tail = jnp.exp(-d * float(CHUNK - 1))
        hop = jnp.exp(-d * float(CHUNK))
        state = jnp.zeros((1, width), jnp.float32)
        for k in range(chunks):
            rows = slice(k * CHUNK, (k + 1) * CHUNK)
            scaled = grow * g_ref[rows, :]
            high = scaled.astype(jnp.bfloat16)
            low = (scaled - high.astype(jnp.float32)).astype(jnp.bfloat16)
            y = jnp.dot(lower, high, preferred_element_type=jnp.float32) + jnp.dot(
                lower, low, preferred_element_type=jnp.float32
            )
            out_ref[rows, :] += shrink * y + after * state
            state = hop * state + tail * y[CHUNK - 1 : CHUNK, :]
        total_ref[pl.ds(r, 1), :] = state
        return carry

    lax.fori_loop(0, d_ref.shape[0], mode, 0)


def packed_conv(packed, residues, decays, parts):
    seg, lanes = packed.shape
    width = lanes // parts
    modes = decays.shape[0]
    weight = residues * jnp.sqrt(-jnp.expm1(-2.0 * decays))
    decays_p = jnp.concatenate([decays] * parts, axis=1)
    weight_p = jnp.concatenate([weight] * parts, axis=1)
    local, ends = pl.pallas_call(
        conv_kernel,
        out_shape=(
            jax.ShapeDtypeStruct((seg, lanes), jnp.float32),
            jax.ShapeDtypeStruct(decays_p.shape, jnp.float32),
        ),
        interpret=INTERPRET,
    )(packed, decays_p, weight_p)
    ends = ends.reshape(modes, parts, width)
    index = jnp.arange(parts)
    lag = index[:, None] - 1 - index[None, :]
    gap = (float(seg) * jnp.maximum(lag, 0).astype(jnp.float32))[None, :, :, None]
    table = jnp.where((lag >= 0)[None, :, :, None], jnp.exp(-decays[:, None, None, :] * gap), 0.0)
    entry = jnp.sum(table * ends[:, None, :, :], axis=2).reshape(modes, lanes)
    steps = jnp.arange(seg, dtype=jnp.float32)
    after = jnp.exp(-decays_p[:, None, :] * (steps[None, :, None] + 1.0))
    return local + jnp.sum((weight_p * entry)[:, None, :] * after, axis=0)


def shards(
    query_input, key_input, value_input, short_filter, residues, decays, skip_gain, head_weight
):
    tokens, chan_width = query_input.shape
    width_v = lax.axis_size("v")
    piece = head_weight.shape[1]
    span = tokens * width_v
    parts = max(1, 128 // piece)
    seg = span // parts
    blocks = width_v // parts
    lanes = parts * piece
    before = from_behind(
        jnp.stack([query_input[-2:], key_input[-2:], value_input[-2:]], axis=0), "v", 1
    )
    key_short = short_pass(key_input, before[1], short_filter[:, 1])
    value_short = short_pass(value_input, before[2], short_filter[:, 2])
    gated_rows = (key_short * value_short).astype(jnp.bfloat16)

    def by_target(values):
        depth = values.shape[0]
        return jnp.transpose(values.reshape(depth, width_v, piece), (1, 0, 2))

    payload = jnp.concatenate(
        [by_target(before[0]), by_target(query_input), by_target(gated_rows)], axis=1
    )
    depth = payload.shape[1]
    columns = lax.all_to_all(payload, "v", split_axis=0, concat_axis=0, tiled=True)
    columns = jnp.transpose(columns.reshape(parts, blocks, depth, piece), (1, 2, 0, 3))
    query_before = columns[0, :2].reshape(2, lanes)
    query_p = columns[:, 2 : 2 + tokens].reshape(seg, lanes)
    gated_p = columns[:, 2 + tokens :].reshape(seg, lanes)
    head = lax.axis_index("v") * piece

    def own(values):
        return lax.dynamic_slice_in_dim(values, head, piece, axis=values.ndim - 1)

    sf = jnp.concatenate([own(short_filter)] * parts, axis=2)
    gain = jnp.concatenate([own(skip_gain)] * parts, axis=0)
    query_short = short_pass(query_p, query_before, sf[:, 0])
    convolved = packed_conv(gated_p, own(residues), own(decays), parts)
    carried = (convolved + gain * gated_p.astype(jnp.float32)).astype(jnp.bfloat16)
    op_p = (query_short * carried.astype(jnp.float32)).astype(jnp.bfloat16)
    following = jnp.concatenate(
        [op_p[:STRIDE, piece:], jnp.zeros((STRIDE, piece), op_p.dtype)], axis=1
    )
    extended = jnp.concatenate([op_p, following], axis=0)
    rows_seg = seg // STRIDE
    early_rows = extended[:seg].reshape(rows_seg, STRIDE, parts, piece)
    late_rows = extended[STRIDE:].reshape(rows_seg, STRIDE, parts, piece)
    partial_sum = jnp.einsum(
        "jisc,ico->sjo", early_rows, head_weight[:STRIDE], preferred_element_type=jnp.float32
    ) + jnp.einsum(
        "jisc,ico->sjo", late_rows, head_weight[STRIDE:], preferred_element_type=jnp.float32
    )
    op_t = jnp.transpose(op_p.reshape(blocks, tokens, parts, piece), (2, 0, 1, 3))
    op_t = op_t.reshape(width_v, tokens, 1, 1, piece)
    sums = partial_sum.astype(jnp.bfloat16).reshape(width_v, -1, 1, 1, piece)
    outgoing = jnp.concatenate([op_t, sums], axis=1)
    incoming = lax.all_to_all(outgoing, "v", split_axis=0, concat_axis=3, tiled=True)[0]
    operator_out = incoming[:tokens].reshape(tokens, chan_width)
    sums = jnp.transpose(incoming[tokens:], (2, 0, 1, 3)).astype(jnp.float32)
    block_sum = jnp.sum(sums.reshape(width_v, tokens // STRIDE, -1), axis=0)
    probe_out = lax.psum_scatter(block_sum, "tp", scatter_dimension=0, tiled=True).astype(
        jnp.bfloat16
    )
    return (operator_out, probe_out)


def solution(mesh):
    seq_size, tp_size = mesh.devices.shape
    width_u = 1
    split = jax.sharding.Mesh(
        mesh.devices.reshape(width_u, seq_size // width_u, tp_size), ("u", "v", "tp")
    )
    seq = ("u", "v")
    placed = (
        P(seq, "tp"),
        P(seq, "tp"),
        P(seq, "tp"),
        P(None, None, "tp"),
        P(None, "tp"),
        P(None, "tp"),
        P("tp"),
        P(None, ("tp", "u", "v"), None),
    )
    return jax.shard_map(
        shards,
        mesh=split,
        in_specs=placed,
        out_specs=(P(seq, "tp"), P(("u", "v", "tp"), None)),
        check_vma=False,
    )
```

```python
import jax
import jax.numpy as jnp
from jax import lax
from jax.experimental import pallas as pl
from jax.sharding import PartitionSpec as P

STRIDE = 16
CHUNK = 128
INTERPRET = False

highest = lax.Precision.HIGHEST


def from_behind(block, axis, distance):
    devices = range(lax.axis_size(axis))
    route = [(i - distance, i) for i in devices if i - distance in devices]
    return lax.ppermute(block, axis, route)


def short_pass(rows, before, tap_weights):
    joined = jnp.concatenate([before, rows], axis=0).astype(jnp.float32)
    row_count = rows.shape[0]
    return (
        tap_weights[0] * joined[2 : 2 + row_count]
        + tap_weights[1] * joined[1 : 1 + row_count]
        + tap_weights[2] * joined[0:row_count]
    )


def conv_kernel(g_ref, d_ref, w_ref, out_ref, total_ref):
    span, width = g_ref.shape
    chunks = span // CHUNK
    row = lax.broadcasted_iota(jnp.int32, (CHUNK, CHUNK), 0)
    col = lax.broadcasted_iota(jnp.int32, (CHUNK, CHUNK), 1)
    lower = (row >= col).astype(jnp.bfloat16)
    steps = lax.broadcasted_iota(jnp.int32, (CHUNK, width), 0).astype(jnp.float32)
    out_ref[...] = jnp.zeros(out_ref.shape, jnp.float32)

    def mode(r, carry):
        d = d_ref[pl.ds(r, 1), :]
        w = w_ref[pl.ds(r, 1), :]
        grow = jnp.exp(d * steps)
        shrink = w * jnp.exp(-d * steps)
        after = w * jnp.exp(-d * (steps + 1.0))
        tail = jnp.exp(-d * float(CHUNK - 1))
        hop = jnp.exp(-d * float(CHUNK))
        state = jnp.zeros((1, width), jnp.float32)
        for k in range(chunks):
            rows = slice(k * CHUNK, (k + 1) * CHUNK)
            scaled = grow * g_ref[rows, :]
            high = scaled.astype(jnp.bfloat16)
            low = (scaled - high.astype(jnp.float32)).astype(jnp.bfloat16)
            y = jnp.dot(lower, high, preferred_element_type=jnp.float32) + jnp.dot(
                lower, low, preferred_element_type=jnp.float32
            )
            out_ref[rows, :] += shrink * y + after * state
            state = hop * state + tail * y[CHUNK - 1 : CHUNK, :]
        total_ref[pl.ds(r, 1), :] = state
        return carry

    lax.fori_loop(0, d_ref.shape[0], mode, 0)


def packed_conv(packed, residues, decays, parts):
    seg, lanes = packed.shape
    width = lanes // parts
    modes = decays.shape[0]
    weight = residues * jnp.sqrt(-jnp.expm1(-2.0 * decays))
    decays_p = jnp.concatenate([decays] * parts, axis=1)
    weight_p = jnp.concatenate([weight] * parts, axis=1)
    local, ends = pl.pallas_call(
        conv_kernel,
        out_shape=(
            jax.ShapeDtypeStruct((seg, lanes), jnp.float32),
            jax.ShapeDtypeStruct(decays_p.shape, jnp.float32),
        ),
        interpret=INTERPRET,
    )(packed, decays_p, weight_p)
    ends = ends.reshape(modes, parts, width)
    index = jnp.arange(parts)
    lag = index[:, None] - 1 - index[None, :]
    gap = (float(seg) * jnp.maximum(lag, 0).astype(jnp.float32))[None, :, :, None]
    table = jnp.where((lag >= 0)[None, :, :, None], jnp.exp(-decays[:, None, None, :] * gap), 0.0)
    entry = jnp.sum(table * ends[:, None, :, :], axis=2).reshape(modes, lanes)
    steps = jnp.arange(seg, dtype=jnp.float32)
    after = jnp.exp(-decays_p[:, None, :] * (steps[None, :, None] + 1.0))
    return local + jnp.sum((weight_p * entry)[:, None, :] * after, axis=0)


def shards(
    query_input, key_input, value_input, short_filter, residues, decays, skip_gain, head_weight
):
    tokens, chan_width = query_input.shape
    width_v = lax.axis_size("v")
    piece = head_weight.shape[1]
    span = tokens * width_v
    parts = max(1, 128 // piece)
    seg = span // parts
    blocks = width_v // parts
    lanes = parts * piece
    before = from_behind(
        jnp.stack([query_input[-2:], key_input[-2:], value_input[-2:]], axis=0), "v", 1
    )
    key_short = short_pass(key_input, before[1], short_filter[:, 1])
    value_short = short_pass(value_input, before[2], short_filter[:, 2])
    gated_rows = (key_short * value_short).astype(jnp.bfloat16)

    def by_target(values):
        depth = values.shape[0]
        return jnp.transpose(values.reshape(depth, width_v, piece), (1, 0, 2))

    payload = jnp.concatenate(
        [by_target(before[0]), by_target(query_input), by_target(gated_rows)], axis=1
    )
    depth = payload.shape[1]
    columns = lax.all_to_all(payload, "v", split_axis=0, concat_axis=0, tiled=True)
    columns = jnp.transpose(columns.reshape(parts, blocks, depth, piece), (1, 2, 0, 3))
    query_before = columns[0, :2].reshape(2, lanes)
    query_p = columns[:, 2 : 2 + tokens].reshape(seg, lanes)
    gated_p = columns[:, 2 + tokens :].reshape(seg, lanes)
    head = lax.axis_index("v") * piece

    def own(values):
        return lax.dynamic_slice_in_dim(values, head, piece, axis=values.ndim - 1)

    sf = jnp.concatenate([own(short_filter)] * parts, axis=2)
    gain = jnp.concatenate([own(skip_gain)] * parts, axis=0)
    query_short = short_pass(query_p, query_before, sf[:, 0])
    convolved = packed_conv(gated_p, own(residues), own(decays), parts)
    carried = (convolved + gain * gated_p.astype(jnp.float32)).astype(jnp.bfloat16)
    op_p = (query_short * carried.astype(jnp.float32)).astype(jnp.bfloat16)
    following = jnp.concatenate(
        [op_p[:STRIDE, piece:], jnp.zeros((STRIDE, piece), op_p.dtype)], axis=1
    )
    extended = jnp.concatenate([op_p, following], axis=0)
    rows_seg = seg // STRIDE
    eye = jnp.eye(parts, dtype=head_weight.dtype)

    def spread(taps):
        return jnp.einsum("ico,ts->itcso", taps, eye).reshape(STRIDE * lanes, parts * taps.shape[2])

    early_rows = extended[:seg].reshape(rows_seg, STRIDE * lanes)
    late_rows = extended[STRIDE:].reshape(rows_seg, STRIDE * lanes)
    by_lane = jnp.dot(
        early_rows, spread(head_weight[:STRIDE]), preferred_element_type=jnp.float32
    ) + jnp.dot(late_rows, spread(head_weight[STRIDE:]), preferred_element_type=jnp.float32)
    per_block = tokens // STRIDE
    partial_sum = jnp.transpose(
        by_lane.reshape(blocks, per_block, parts, -1), (2, 0, 1, 3)
    ).reshape(width_v, per_block, -1)
    op_t = jnp.transpose(op_p.reshape(blocks, tokens, parts, piece), (2, 0, 1, 3))
    op_t = op_t.reshape(width_v, tokens, 1, 1, piece)
    sums = partial_sum.astype(jnp.bfloat16).reshape(width_v, -1, 1, 1, piece)
    outgoing = jnp.concatenate([op_t, sums], axis=1)
    incoming = lax.all_to_all(outgoing, "v", split_axis=0, concat_axis=3, tiled=True)[0]
    operator_out = incoming[:tokens].reshape(tokens, chan_width)
    sums = jnp.transpose(incoming[tokens:], (2, 0, 1, 3)).astype(jnp.float32)
    block_sum = jnp.sum(sums.reshape(width_v, tokens // STRIDE, -1), axis=0)
    probe_out = lax.psum_scatter(block_sum, "tp", scatter_dimension=0, tiled=True).astype(
        jnp.bfloat16
    )
    return (operator_out, probe_out)


def solution(mesh):
    seq_size, tp_size = mesh.devices.shape
    width_u = 1
    split = jax.sharding.Mesh(
        mesh.devices.reshape(width_u, seq_size // width_u, tp_size), ("u", "v", "tp")
    )
    seq = ("u", "v")
    placed = (
        P(seq, "tp"),
        P(seq, "tp"),
        P(seq, "tp"),
        P(None, None, "tp"),
        P(None, "tp"),
        P(None, "tp"),
        P("tp"),
        P(None, ("tp", "u", "v"), None),
    )
    return jax.shard_map(
        shards,
        mesh=split,
        in_specs=placed,
        out_specs=(P(seq, "tp"), P(("u", "v", "tp"), None)),
        check_vma=False,
    )
```

```python
import jax
import jax.numpy as jnp
from jax import lax
from jax.experimental import pallas as pl
from jax.sharding import PartitionSpec as P

STRIDE = 16
CHUNK = 128
INTERPRET = False

highest = lax.Precision.HIGHEST


def from_behind(block, axis, distance):
    devices = range(lax.axis_size(axis))
    route = [(i - distance, i) for i in devices if i - distance in devices]
    return lax.ppermute(block, axis, route)


def short_pass(rows, before, tap_weights):
    joined = jnp.concatenate([before, rows], axis=0).astype(jnp.float32)
    row_count = rows.shape[0]
    return (
        tap_weights[0] * joined[2 : 2 + row_count]
        + tap_weights[1] * joined[1 : 1 + row_count]
        + tap_weights[2] * joined[0:row_count]
    )


def conv_kernel(g_ref, d_ref, w_ref, out_ref, total_ref):
    span, width = g_ref.shape
    chunks = span // CHUNK
    row = lax.broadcasted_iota(jnp.int32, (CHUNK, CHUNK), 0)
    col = lax.broadcasted_iota(jnp.int32, (CHUNK, CHUNK), 1)
    lower = (row >= col).astype(jnp.bfloat16)
    steps = lax.broadcasted_iota(jnp.int32, (CHUNK, width), 0).astype(jnp.float32)
    out_ref[...] = jnp.zeros(out_ref.shape, jnp.float32)

    def mode(r, carry):
        d = d_ref[pl.ds(r, 1), :]
        w = w_ref[pl.ds(r, 1), :]
        grow = jnp.exp(d * steps)
        shrink = w * jnp.exp(-d * steps)
        after = w * jnp.exp(-d * (steps + 1.0))
        tail = jnp.exp(-d * float(CHUNK - 1))
        hop = jnp.exp(-d * float(CHUNK))
        state = jnp.zeros((1, width), jnp.float32)
        for k in range(chunks):
            rows = slice(k * CHUNK, (k + 1) * CHUNK)
            scaled = grow * g_ref[rows, :]
            high = scaled.astype(jnp.bfloat16)
            low = (scaled - high.astype(jnp.float32)).astype(jnp.bfloat16)
            y = jnp.dot(lower, high, preferred_element_type=jnp.float32) + jnp.dot(
                lower, low, preferred_element_type=jnp.float32
            )
            out_ref[rows, :] += shrink * y + after * state
            state = hop * state + tail * y[CHUNK - 1 : CHUNK, :]
        total_ref[pl.ds(r, 1), :] = state
        return carry

    lax.fori_loop(0, d_ref.shape[0], mode, 0)


def packed_conv(packed, residues, decays, parts):
    seg, lanes = packed.shape
    width = lanes // parts
    modes = decays.shape[0]
    weight = residues * jnp.sqrt(-jnp.expm1(-2.0 * decays))
    decays_p = jnp.concatenate([decays] * parts, axis=1)
    weight_p = jnp.concatenate([weight] * parts, axis=1)
    local, ends = pl.pallas_call(
        conv_kernel,
        out_shape=(
            jax.ShapeDtypeStruct((seg, lanes), jnp.float32),
            jax.ShapeDtypeStruct(decays_p.shape, jnp.float32),
        ),
        interpret=INTERPRET,
    )(packed, decays_p, weight_p)
    ends = ends.reshape(modes, parts, width)
    index = jnp.arange(parts)
    lag = index[:, None] - 1 - index[None, :]
    gap = (float(seg) * jnp.maximum(lag, 0).astype(jnp.float32))[None, :, :, None]
    table = jnp.where((lag >= 0)[None, :, :, None], jnp.exp(-decays[:, None, None, :] * gap), 0.0)
    entry = jnp.sum(table * ends[:, None, :, :], axis=2).reshape(modes, lanes)
    steps = jnp.arange(seg, dtype=jnp.float32)
    after = jnp.exp(-decays_p[:, None, :] * (steps[None, :, None] + 1.0))
    return local + jnp.sum((weight_p * entry)[:, None, :] * after, axis=0)


def shards(
    query_input, key_input, value_input, short_filter, residues, decays, skip_gain, head_weight
):
    tokens, chan_width = query_input.shape
    width_v = lax.axis_size("v")
    piece = head_weight.shape[1]
    span = tokens * width_v
    parts = max(1, 128 // piece)
    seg = span // parts
    blocks = width_v // parts
    lanes = parts * piece
    def by_target(values):
        depth = values.shape[0]
        return jnp.transpose(values.reshape(depth, width_v, piece), (1, 0, 2))

    payload = jnp.concatenate(
        [by_target(key_input), by_target(value_input), by_target(query_input)], axis=1
    )
    depth = payload.shape[1]
    columns = lax.all_to_all(payload, "v", split_axis=0, concat_axis=0, tiled=True)
    columns = jnp.transpose(columns.reshape(parts, blocks, depth, piece), (1, 2, 0, 3))
    key_p, value_p, query_p = (
        columns[:, i * tokens : (i + 1) * tokens].reshape(seg, lanes) for i in range(3)
    )

    def behind(values):
        lead = jnp.zeros((2, piece), values.dtype)
        return jnp.concatenate([lead, values[-2:, : lanes - piece]], axis=1)

    head = lax.axis_index("v") * piece

    def own(values):
        return lax.dynamic_slice_in_dim(values, head, piece, axis=values.ndim - 1)

    sf = jnp.concatenate([own(short_filter)] * parts, axis=2)
    gain = jnp.concatenate([own(skip_gain)] * parts, axis=0)
    key_short = short_pass(key_p, behind(key_p), sf[:, 1])
    value_short = short_pass(value_p, behind(value_p), sf[:, 2])
    gated_p = (key_short * value_short).astype(jnp.bfloat16)
    query_short = short_pass(query_p, behind(query_p), sf[:, 0])
    convolved = packed_conv(gated_p, own(residues), own(decays), parts)
    carried = (convolved + gain * gated_p.astype(jnp.float32)).astype(jnp.bfloat16)
    op_p = (query_short * carried.astype(jnp.float32)).astype(jnp.bfloat16)
    following = jnp.concatenate(
        [op_p[:STRIDE, piece:], jnp.zeros((STRIDE, piece), op_p.dtype)], axis=1
    )
    extended = jnp.concatenate([op_p, following], axis=0)
    rows_seg = seg // STRIDE
    early_rows = extended[:seg].reshape(rows_seg, STRIDE, parts, piece)
    late_rows = extended[STRIDE:].reshape(rows_seg, STRIDE, parts, piece)
    partial_sum = jnp.einsum(
        "jisc,ico->sjo", early_rows, head_weight[:STRIDE], preferred_element_type=jnp.float32
    ) + jnp.einsum(
        "jisc,ico->sjo", late_rows, head_weight[STRIDE:], preferred_element_type=jnp.float32
    )
    op_t = jnp.transpose(op_p.reshape(blocks, tokens, parts, piece), (2, 0, 1, 3))
    op_t = op_t.reshape(width_v, tokens, 1, 1, piece)
    sums = partial_sum.astype(jnp.bfloat16).reshape(width_v, -1, 1, 1, piece)
    outgoing = jnp.concatenate([op_t, sums], axis=1)
    incoming = lax.all_to_all(outgoing, "v", split_axis=0, concat_axis=3, tiled=True)[0]
    operator_out = incoming[:tokens].reshape(tokens, chan_width)
    sums = jnp.transpose(incoming[tokens:], (2, 0, 1, 3)).astype(jnp.float32)
    block_sum = jnp.sum(sums.reshape(width_v, tokens // STRIDE, -1), axis=0)
    probe_out = lax.psum_scatter(block_sum, "tp", scatter_dimension=0, tiled=True).astype(
        jnp.bfloat16
    )
    return (operator_out, probe_out)


def solution(mesh):
    seq_size, tp_size = mesh.devices.shape
    width_u = 1
    split = jax.sharding.Mesh(
        mesh.devices.reshape(width_u, seq_size // width_u, tp_size), ("u", "v", "tp")
    )
    seq = ("u", "v")
    placed = (
        P(seq, "tp"),
        P(seq, "tp"),
        P(seq, "tp"),
        P(None, None, "tp"),
        P(None, "tp"),
        P(None, "tp"),
        P("tp"),
        P(None, ("tp", "u", "v"), None),
    )
    return jax.shard_map(
        shards,
        mesh=split,
        in_specs=placed,
        out_specs=(P(seq, "tp"), P(("u", "v", "tp"), None)),
        check_vma=False,
    )
```

```python
import jax
import jax.numpy as jnp
from jax import lax
from jax.experimental import pallas as pl
from jax.sharding import PartitionSpec as P

STRIDE = 16
CHUNK = 128
INTERPRET = False

highest = lax.Precision.HIGHEST


def from_behind(block, axis, distance):
    devices = range(lax.axis_size(axis))
    route = [(i - distance, i) for i in devices if i - distance in devices]
    return lax.ppermute(block, axis, route)


def short_pass(rows, before, tap_weights):
    joined = jnp.concatenate([before, rows], axis=0).astype(jnp.float32)
    row_count = rows.shape[0]
    return (
        tap_weights[0] * joined[2 : 2 + row_count]
        + tap_weights[1] * joined[1 : 1 + row_count]
        + tap_weights[2] * joined[0:row_count]
    )


def conv_kernel(g_ref, d_ref, w_ref, out_ref, total_ref):
    span, width = g_ref.shape
    chunks = span // CHUNK
    row = lax.broadcasted_iota(jnp.int32, (CHUNK, CHUNK), 0)
    col = lax.broadcasted_iota(jnp.int32, (CHUNK, CHUNK), 1)
    lower = (row >= col).astype(jnp.bfloat16)
    steps = lax.broadcasted_iota(jnp.int32, (CHUNK, width), 0).astype(jnp.float32)
    out_ref[...] = jnp.zeros(out_ref.shape, jnp.float32)

    def mode(r, carry):
        d = d_ref[pl.ds(r, 1), :]
        w = w_ref[pl.ds(r, 1), :]
        grow = jnp.exp(d * steps)
        shrink = w * jnp.exp(-d * steps)
        after = w * jnp.exp(-d * (steps + 1.0))
        tail = jnp.exp(-d * float(CHUNK - 1))
        hop = jnp.exp(-d * float(CHUNK))
        state = jnp.zeros((1, width), jnp.float32)
        for k in range(chunks):
            rows = slice(k * CHUNK, (k + 1) * CHUNK)
            scaled = grow * g_ref[rows, :]
            high = scaled.astype(jnp.bfloat16)
            low = (scaled - high.astype(jnp.float32)).astype(jnp.bfloat16)
            y = jnp.dot(lower, high, preferred_element_type=jnp.float32) + jnp.dot(
                lower, low, preferred_element_type=jnp.float32
            )
            out_ref[rows, :] += shrink * y + after * state
            state = hop * state + tail * y[CHUNK - 1 : CHUNK, :]
        total_ref[pl.ds(r, 1), :] = state
        return carry

    lax.fori_loop(0, d_ref.shape[0], mode, 0)


def packed_conv(packed, residues, decays, parts):
    seg, lanes = packed.shape
    width = lanes // parts
    modes = decays.shape[0]
    weight = residues * jnp.sqrt(-jnp.expm1(-2.0 * decays))
    decays_p = jnp.concatenate([decays] * parts, axis=1)
    weight_p = jnp.concatenate([weight] * parts, axis=1)
    local, ends = pl.pallas_call(
        conv_kernel,
        out_shape=(
            jax.ShapeDtypeStruct((seg, lanes), jnp.float32),
            jax.ShapeDtypeStruct(decays_p.shape, jnp.float32),
        ),
        interpret=INTERPRET,
    )(packed, decays_p, weight_p)
    ends = ends.reshape(modes, parts, width)
    index = jnp.arange(parts)
    lag = index[:, None] - 1 - index[None, :]
    gap = (float(seg) * jnp.maximum(lag, 0).astype(jnp.float32))[None, :, :, None]
    table = jnp.where((lag >= 0)[None, :, :, None], jnp.exp(-decays[:, None, None, :] * gap), 0.0)
    entry = jnp.sum(table * ends[:, None, :, :], axis=2).reshape(modes, lanes)
    steps = jnp.arange(seg, dtype=jnp.float32)
    after = jnp.exp(-decays_p[:, None, :] * (steps[None, :, None] + 1.0))
    return local + jnp.sum((weight_p * entry)[:, None, :] * after, axis=0)


def shards(
    query_input, key_input, value_input, short_filter, residues, decays, skip_gain, head_weight
):
    tokens, chan_width = query_input.shape
    width_v = lax.axis_size("v")
    piece = head_weight.shape[1]
    span = tokens * width_v
    parts = max(1, 128 // piece)
    seg = span // parts
    blocks = width_v // parts
    lanes = parts * piece
    def by_target(values):
        depth = values.shape[0]
        return jnp.transpose(values.reshape(depth, width_v, piece), (1, 0, 2))

    payload = jnp.concatenate(
        [by_target(key_input), by_target(value_input), by_target(query_input)], axis=1
    )
    depth = payload.shape[1]
    columns = lax.all_to_all(payload, "v", split_axis=0, concat_axis=0, tiled=True)
    columns = jnp.transpose(columns.reshape(parts, blocks, depth, piece), (1, 2, 0, 3))
    key_p, value_p, query_p = (
        columns[:, i * tokens : (i + 1) * tokens].reshape(seg, lanes) for i in range(3)
    )

    def behind(values):
        lead = jnp.zeros((2, piece), values.dtype)
        return jnp.concatenate([lead, values[-2:, : lanes - piece]], axis=1)

    head = lax.axis_index("v") * piece

    def own(values):
        return lax.dynamic_slice_in_dim(values, head, piece, axis=values.ndim - 1)

    sf = jnp.concatenate([own(short_filter)] * parts, axis=2)
    gain = jnp.concatenate([own(skip_gain)] * parts, axis=0)
    key_short = short_pass(key_p, behind(key_p), sf[:, 1])
    value_short = short_pass(value_p, behind(value_p), sf[:, 2])
    gated_p = (key_short * value_short).astype(jnp.bfloat16)
    query_short = short_pass(query_p, behind(query_p), sf[:, 0])
    convolved = packed_conv(gated_p, own(residues), own(decays), parts)
    carried = (convolved + gain * gated_p.astype(jnp.float32)).astype(jnp.bfloat16)
    op_p = (query_short * carried.astype(jnp.float32)).astype(jnp.bfloat16)
    following = jnp.concatenate(
        [op_p[:STRIDE, piece:], jnp.zeros((STRIDE, piece), op_p.dtype)], axis=1
    )
    extended = jnp.concatenate([op_p, following], axis=0)
    rows_seg = seg // STRIDE
    early_rows = extended[:seg].reshape(rows_seg, STRIDE, parts, piece)
    late_rows = extended[STRIDE:].reshape(rows_seg, STRIDE, parts, piece)
    partial_sum = jnp.einsum(
        "jisc,ico->sjo", early_rows, head_weight[:STRIDE], preferred_element_type=jnp.float32
    ) + jnp.einsum(
        "jisc,ico->sjo", late_rows, head_weight[STRIDE:], preferred_element_type=jnp.float32
    )
    op_t = jnp.transpose(op_p.reshape(blocks, tokens, parts, piece), (2, 0, 1, 3))
    op_t = op_t.reshape(width_v, tokens, 1, piece)
    incoming = lax.all_to_all(op_t, "v", split_axis=0, concat_axis=2, tiled=True)[0]
    operator_out = incoming.reshape(tokens, chan_width)
    block_sum = lax.psum_scatter(
        partial_sum.reshape(span // STRIDE, -1), "v", scatter_dimension=0, tiled=True
    )
    probe_out = lax.psum_scatter(block_sum, "tp", scatter_dimension=0, tiled=True).astype(
        jnp.bfloat16
    )
    return (operator_out, probe_out)


def solution(mesh):
    seq_size, tp_size = mesh.devices.shape
    width_u = 1
    split = jax.sharding.Mesh(
        mesh.devices.reshape(width_u, seq_size // width_u, tp_size), ("u", "v", "tp")
    )
    seq = ("u", "v")
    placed = (
        P(seq, "tp"),
        P(seq, "tp"),
        P(seq, "tp"),
        P(None, None, "tp"),
        P(None, "tp"),
        P(None, "tp"),
        P("tp"),
        P(None, ("tp", "u", "v"), None),
    )
    return jax.shard_map(
        shards,
        mesh=split,
        in_specs=placed,
        out_specs=(P(seq, "tp"), P(("u", "v", "tp"), None)),
        check_vma=False,
    )
```

```python
import jax
import jax.numpy as jnp
from jax import lax
from jax.experimental import pallas as pl
from jax.sharding import PartitionSpec as P

STRIDE = 16
CHUNK = 128
INTERPRET = False

highest = lax.Precision.HIGHEST


def from_behind(block, axis, distance):
    devices = range(lax.axis_size(axis))
    route = [(i - distance, i) for i in devices if i - distance in devices]
    return lax.ppermute(block, axis, route)


def short_pass(rows, before, tap_weights):
    joined = jnp.concatenate([before, rows], axis=0).astype(jnp.float32)
    row_count = rows.shape[0]
    return (
        tap_weights[0] * joined[2 : 2 + row_count]
        + tap_weights[1] * joined[1 : 1 + row_count]
        + tap_weights[2] * joined[0:row_count]
    )


def conv_kernel(g_ref, d_ref, w_ref, out_ref, total_ref):
    span, width = g_ref.shape
    chunks = span // CHUNK
    row = lax.broadcasted_iota(jnp.int32, (CHUNK, CHUNK), 0)
    col = lax.broadcasted_iota(jnp.int32, (CHUNK, CHUNK), 1)
    lower = (row >= col).astype(jnp.bfloat16)
    steps = lax.broadcasted_iota(jnp.int32, (CHUNK, width), 0).astype(jnp.float32)
    out_ref[...] = jnp.zeros(out_ref.shape, jnp.float32)

    def mode(r, carry):
        d = d_ref[pl.ds(r, 1), :]
        w = w_ref[pl.ds(r, 1), :]
        grow = jnp.exp(d * steps)
        shrink = w * jnp.exp(-d * steps)
        after = w * jnp.exp(-d * (steps + 1.0))
        tail = jnp.exp(-d * float(CHUNK - 1))
        hop = jnp.exp(-d * float(CHUNK))
        state = jnp.zeros((1, width), jnp.float32)
        for k in range(chunks):
            rows = slice(k * CHUNK, (k + 1) * CHUNK)
            scaled = grow * g_ref[rows, :]
            high = scaled.astype(jnp.bfloat16)
            low = (scaled - high.astype(jnp.float32)).astype(jnp.bfloat16)
            y = jnp.dot(lower, high, preferred_element_type=jnp.float32) + jnp.dot(
                lower, low, preferred_element_type=jnp.float32
            )
            out_ref[rows, :] += shrink * y + after * state
            state = hop * state + tail * y[CHUNK - 1 : CHUNK, :]
        total_ref[pl.ds(r, 1), :] = state
        return carry

    lax.fori_loop(0, d_ref.shape[0], mode, 0)


def packed_conv(packed, residues, decays, parts):
    seg, lanes = packed.shape
    width = lanes // parts
    modes = decays.shape[0]
    weight = residues * jnp.sqrt(-jnp.expm1(-2.0 * decays))
    decays_p = jnp.concatenate([decays] * parts, axis=1)
    weight_p = jnp.concatenate([weight] * parts, axis=1)
    local, ends = pl.pallas_call(
        conv_kernel,
        out_shape=(
            jax.ShapeDtypeStruct((seg, lanes), jnp.float32),
            jax.ShapeDtypeStruct(decays_p.shape, jnp.float32),
        ),
        interpret=INTERPRET,
    )(packed, decays_p, weight_p)
    ends = ends.reshape(modes, parts, width)
    index = jnp.arange(parts)
    lag = index[:, None] - 1 - index[None, :]
    gap = (float(seg) * jnp.maximum(lag, 0).astype(jnp.float32))[None, :, :, None]
    table = jnp.where((lag >= 0)[None, :, :, None], jnp.exp(-decays[:, None, None, :] * gap), 0.0)
    entry = jnp.sum(table * ends[:, None, :, :], axis=2).reshape(modes, lanes)
    steps = jnp.arange(seg, dtype=jnp.float32)
    after = jnp.exp(-decays_p[:, None, :] * (steps[None, :, None] + 1.0))
    return local + jnp.sum((weight_p * entry)[:, None, :] * after, axis=0)


def shards(
    query_input, key_input, value_input, short_filter, residues, decays, skip_gain, head_weight
):
    tokens, chan_width = query_input.shape
    width_v = lax.axis_size("v")
    piece = head_weight.shape[1]
    span = tokens * width_v
    parts = max(1, 128 // piece)
    seg = span // parts
    blocks = width_v // parts
    lanes = parts * piece
    def by_target(values):
        depth = values.shape[0]
        return jnp.transpose(values.reshape(depth, width_v, piece), (1, 0, 2))

    payload = jnp.concatenate(
        [by_target(key_input), by_target(value_input), by_target(query_input)], axis=1
    )
    depth = payload.shape[1]
    columns = lax.all_to_all(payload, "v", split_axis=0, concat_axis=0, tiled=True)
    columns = jnp.transpose(columns.reshape(parts, blocks, depth, piece), (1, 2, 0, 3))
    key_p, value_p, query_p = (
        columns[:, i * tokens : (i + 1) * tokens].reshape(seg, lanes) for i in range(3)
    )

    def behind(values):
        lead = jnp.zeros((2, piece), values.dtype)
        return jnp.concatenate([lead, values[-2:, : lanes - piece]], axis=1)

    head = lax.axis_index("v") * piece

    def own(values):
        return lax.dynamic_slice_in_dim(values, head, piece, axis=values.ndim - 1)

    sf = jnp.concatenate([own(short_filter)] * parts, axis=2)
    gain = jnp.concatenate([own(skip_gain)] * parts, axis=0)
    key_short = short_pass(key_p, behind(key_p), sf[:, 1])
    value_short = short_pass(value_p, behind(value_p), sf[:, 2])
    gated_p = (key_short * value_short).astype(jnp.bfloat16)
    query_short = short_pass(query_p, behind(query_p), sf[:, 0])
    convolved = packed_conv(gated_p, own(residues), own(decays), parts)
    carried = (convolved + gain * gated_p.astype(jnp.float32)).astype(jnp.bfloat16)
    op_p = (query_short * carried.astype(jnp.float32)).astype(jnp.bfloat16)
    following = jnp.concatenate(
        [op_p[:STRIDE, piece:], jnp.zeros((STRIDE, piece), op_p.dtype)], axis=1
    )
    extended = jnp.concatenate([op_p, following], axis=0)
    rows_seg = seg // STRIDE
    eye = jnp.eye(parts, dtype=head_weight.dtype)

    def spread(taps):
        return jnp.einsum("ico,ts->itcso", taps, eye).reshape(STRIDE * lanes, parts * taps.shape[2])

    early_rows = extended[:seg].reshape(rows_seg, STRIDE * lanes)
    late_rows = extended[STRIDE:].reshape(rows_seg, STRIDE * lanes)
    by_lane = jnp.dot(
        early_rows, spread(head_weight[:STRIDE]), preferred_element_type=jnp.float32
    ) + jnp.dot(late_rows, spread(head_weight[STRIDE:]), preferred_element_type=jnp.float32)
    per_block = tokens // STRIDE
    partial_sum = jnp.transpose(
        by_lane.reshape(blocks, per_block, parts, -1), (2, 0, 1, 3)
    ).reshape(width_v, per_block, -1)
    op_t = jnp.transpose(op_p.reshape(blocks, tokens, parts, piece), (2, 0, 1, 3))
    op_t = op_t.reshape(width_v, tokens, 1, 1, piece)
    sums = partial_sum.astype(jnp.bfloat16).reshape(width_v, -1, 1, 1, piece)
    outgoing = jnp.concatenate([op_t, sums], axis=1)
    incoming = lax.all_to_all(outgoing, "v", split_axis=0, concat_axis=3, tiled=True)[0]
    operator_out = incoming[:tokens].reshape(tokens, chan_width)
    sums = jnp.transpose(incoming[tokens:], (2, 0, 1, 3)).astype(jnp.float32)
    block_sum = jnp.sum(sums.reshape(width_v, tokens // STRIDE, -1), axis=0)
    probe_out = lax.psum_scatter(block_sum, "tp", scatter_dimension=0, tiled=True).astype(
        jnp.bfloat16
    )
    return (operator_out, probe_out)


def solution(mesh):
    seq_size, tp_size = mesh.devices.shape
    width_u = 1
    split = jax.sharding.Mesh(
        mesh.devices.reshape(width_u, seq_size // width_u, tp_size), ("u", "v", "tp")
    )
    seq = ("u", "v")
    placed = (
        P(seq, "tp"),
        P(seq, "tp"),
        P(seq, "tp"),
        P(None, None, "tp"),
        P(None, "tp"),
        P(None, "tp"),
        P("tp"),
        P(None, ("tp", "u", "v"), None),
    )
    return jax.shard_map(
        shards,
        mesh=split,
        in_specs=placed,
        out_specs=(P(seq, "tp"), P(("u", "v", "tp"), None)),
        check_vma=False,
    )
```

```python
import jax
import jax.numpy as jnp
from jax import lax
from jax.experimental import pallas as pl
from jax.sharding import PartitionSpec as P

STRIDE = 16
CHUNK = 128
INTERPRET = False

highest = lax.Precision.HIGHEST


def from_behind(block, axis, distance):
    devices = range(lax.axis_size(axis))
    route = [(i - distance, i) for i in devices if i - distance in devices]
    return lax.ppermute(block, axis, route)


def short_pass(rows, before, tap_weights):
    joined = jnp.concatenate([before, rows], axis=0).astype(jnp.float32)
    row_count = rows.shape[0]
    return (
        tap_weights[0] * joined[2 : 2 + row_count]
        + tap_weights[1] * joined[1 : 1 + row_count]
        + tap_weights[2] * joined[0:row_count]
    )


def conv_kernel(g_ref, d_ref, w_ref, out_ref, total_ref):
    span, width = g_ref.shape
    chunks = span // CHUNK
    row = lax.broadcasted_iota(jnp.int32, (CHUNK, CHUNK), 0)
    col = lax.broadcasted_iota(jnp.int32, (CHUNK, CHUNK), 1)
    lower = (row >= col).astype(jnp.bfloat16)
    steps = lax.broadcasted_iota(jnp.int32, (CHUNK, width), 0).astype(jnp.float32)
    out_ref[...] = jnp.zeros(out_ref.shape, jnp.float32)

    def mode(r, carry):
        d = d_ref[pl.ds(r, 1), :]
        w = w_ref[pl.ds(r, 1), :]
        grow = jnp.exp(d * steps)
        shrink = w * jnp.exp(-d * steps)
        step = jnp.exp(-d)
        tail = jnp.exp(-d * float(CHUNK - 1))
        hop = jnp.exp(-d * float(CHUNK))
        state = jnp.zeros((1, width), jnp.float32)
        for k in range(chunks):
            rows = slice(k * CHUNK, (k + 1) * CHUNK)
            scaled = grow * g_ref[rows, :]
            high = scaled.astype(jnp.bfloat16)
            low = (scaled - high.astype(jnp.float32)).astype(jnp.bfloat16)
            y = jnp.dot(lower, high, preferred_element_type=jnp.float32) + jnp.dot(
                lower, low, preferred_element_type=jnp.float32
            )
            out_ref[rows, :] += shrink * (y + step * state)
            state = hop * state + tail * y[CHUNK - 1 : CHUNK, :]
        total_ref[pl.ds(r, 1), :] = state
        return carry

    lax.fori_loop(0, d_ref.shape[0], mode, 0)


def packed_conv(packed, residues, decays, parts):
    seg, lanes = packed.shape
    width = lanes // parts
    modes = decays.shape[0]
    weight = residues * jnp.sqrt(-jnp.expm1(-2.0 * decays))
    decays_p = jnp.concatenate([decays] * parts, axis=1)
    weight_p = jnp.concatenate([weight] * parts, axis=1)
    local, ends = pl.pallas_call(
        conv_kernel,
        out_shape=(
            jax.ShapeDtypeStruct((seg, lanes), jnp.float32),
            jax.ShapeDtypeStruct(decays_p.shape, jnp.float32),
        ),
        interpret=INTERPRET,
    )(packed, decays_p, weight_p)
    ends = ends.reshape(modes, parts, width)
    index = jnp.arange(parts)
    lag = index[:, None] - 1 - index[None, :]
    gap = (float(seg) * jnp.maximum(lag, 0).astype(jnp.float32))[None, :, :, None]
    table = jnp.where((lag >= 0)[None, :, :, None], jnp.exp(-decays[:, None, None, :] * gap), 0.0)
    entry = jnp.sum(table * ends[:, None, :, :], axis=2).reshape(modes, lanes)
    steps = jnp.arange(seg, dtype=jnp.float32)
    after = jnp.exp(-decays_p[:, None, :] * (steps[None, :, None] + 1.0))
    return local + jnp.sum((weight_p * entry)[:, None, :] * after, axis=0)


def shards(
    query_input, key_input, value_input, short_filter, residues, decays, skip_gain, head_weight
):
    tokens, chan_width = query_input.shape
    width_v = lax.axis_size("v")
    piece = head_weight.shape[1]
    span = tokens * width_v
    parts = max(1, 128 // piece)
    seg = span // parts
    blocks = width_v // parts
    lanes = parts * piece
    def by_target(values):
        depth = values.shape[0]
        return jnp.transpose(values.reshape(depth, width_v, piece), (1, 0, 2))

    payload = jnp.stack([key_input, value_input, query_input], axis=0)
    payload = jnp.transpose(payload.reshape(3, tokens, width_v, piece), (2, 0, 1, 3))
    payload = payload.reshape(width_v, 3 * tokens, piece)
    depth = payload.shape[1]
    columns = lax.all_to_all(payload, "v", split_axis=0, concat_axis=0, tiled=True)
    columns = jnp.transpose(columns.reshape(parts, blocks, depth, piece), (1, 2, 0, 3))
    key_p, value_p, query_p = (
        columns[:, i * tokens : (i + 1) * tokens].reshape(seg, lanes) for i in range(3)
    )

    def behind(values):
        lead = jnp.zeros((2, piece), values.dtype)
        return jnp.concatenate([lead, values[-2:, : lanes - piece]], axis=1)

    head = lax.axis_index("v") * piece

    def own(values):
        return lax.dynamic_slice_in_dim(values, head, piece, axis=values.ndim - 1)

    sf = jnp.concatenate([own(short_filter)] * parts, axis=2)
    gain = jnp.concatenate([own(skip_gain)] * parts, axis=0)
    key_short = short_pass(key_p, behind(key_p), sf[:, 1])
    value_short = short_pass(value_p, behind(value_p), sf[:, 2])
    gated_p = (key_short * value_short).astype(jnp.bfloat16)
    query_short = short_pass(query_p, behind(query_p), sf[:, 0])
    convolved = packed_conv(gated_p, own(residues), own(decays), parts)
    carried = (convolved + gain * gated_p.astype(jnp.float32)).astype(jnp.bfloat16)
    op_p = (query_short * carried.astype(jnp.float32)).astype(jnp.bfloat16)
    following = jnp.concatenate(
        [op_p[:STRIDE, piece:], jnp.zeros((STRIDE, piece), op_p.dtype)], axis=1
    )
    extended = jnp.concatenate([op_p, following], axis=0)
    rows_seg = seg // STRIDE
    eye = jnp.eye(parts, dtype=head_weight.dtype)

    def spread(taps):
        return jnp.einsum("ico,ts->itcso", taps, eye).reshape(STRIDE * lanes, parts * taps.shape[2])

    early_rows = extended[:seg].reshape(rows_seg, STRIDE * lanes)
    late_rows = extended[STRIDE:].reshape(rows_seg, STRIDE * lanes)
    by_lane = jnp.dot(
        early_rows, spread(head_weight[:STRIDE]), preferred_element_type=jnp.float32
    ) + jnp.dot(late_rows, spread(head_weight[STRIDE:]), preferred_element_type=jnp.float32)
    per_block = tokens // STRIDE
    partial_sum = jnp.transpose(
        by_lane.reshape(blocks, per_block, parts, -1), (2, 0, 1, 3)
    ).reshape(width_v, per_block, -1)
    op_t = jnp.transpose(op_p.reshape(blocks, tokens, parts, piece), (2, 0, 1, 3))
    op_t = op_t.reshape(width_v, tokens, 1, 1, piece)
    sums = partial_sum.astype(jnp.bfloat16).reshape(width_v, -1, 1, 1, piece)
    outgoing = jnp.concatenate([op_t, sums], axis=1)
    incoming = lax.all_to_all(outgoing, "v", split_axis=0, concat_axis=3, tiled=True)[0]
    operator_out = incoming[:tokens].reshape(tokens, chan_width)
    sums = jnp.transpose(incoming[tokens:], (2, 0, 1, 3)).astype(jnp.float32)
    block_sum = jnp.sum(sums.reshape(width_v, tokens // STRIDE, -1), axis=0)
    probe_out = lax.psum_scatter(block_sum, "tp", scatter_dimension=0, tiled=True).astype(
        jnp.bfloat16
    )
    return (operator_out, probe_out)


def solution(mesh):
    seq_size, tp_size = mesh.devices.shape
    width_u = 1
    split = jax.sharding.Mesh(
        mesh.devices.reshape(width_u, seq_size // width_u, tp_size), ("u", "v", "tp")
    )
    seq = ("u", "v")
    placed = (
        P(seq, "tp"),
        P(seq, "tp"),
        P(seq, "tp"),
        P(None, None, "tp"),
        P(None, "tp"),
        P(None, "tp"),
        P("tp"),
        P(None, ("tp", "u", "v"), None),
    )
    return jax.shard_map(
        shards,
        mesh=split,
        in_specs=placed,
        out_specs=(P(seq, "tp"), P(("u", "v", "tp"), None)),
        check_vma=False,
    )
```

```python
import jax
import jax.numpy as jnp
from jax import lax
from jax.experimental import pallas as pl
from jax.sharding import PartitionSpec as P

STRIDE = 16
CHUNK = 128
INTERPRET = False

highest = lax.Precision.HIGHEST


def from_behind(block, axis, distance):
    devices = range(lax.axis_size(axis))
    route = [(i - distance, i) for i in devices if i - distance in devices]
    return lax.ppermute(block, axis, route)


def short_pass(rows, before, tap_weights):
    joined = jnp.concatenate([before, rows], axis=0).astype(jnp.float32)
    row_count = rows.shape[0]
    return (
        tap_weights[0] * joined[2 : 2 + row_count]
        + tap_weights[1] * joined[1 : 1 + row_count]
        + tap_weights[2] * joined[0:row_count]
    )


def conv_kernel(g_ref, d_ref, w_ref, out_ref, total_ref):
    span, width = g_ref.shape
    chunks = span // CHUNK
    row = lax.broadcasted_iota(jnp.int32, (CHUNK, CHUNK), 0)
    col = lax.broadcasted_iota(jnp.int32, (CHUNK, CHUNK), 1)
    lower = (row >= col).astype(jnp.bfloat16)
    steps = lax.broadcasted_iota(jnp.int32, (CHUNK, width), 0).astype(jnp.float32)
    out_ref[...] = jnp.zeros(out_ref.shape, jnp.float32)

    def mode(r, carry):
        d = d_ref[pl.ds(r, 1), :]
        w = w_ref[pl.ds(r, 1), :]
        grow = jnp.exp(d * steps)
        shrink = w * jnp.exp(-d * steps)
        after = w * jnp.exp(-d * (steps + 1.0))
        tail = jnp.exp(-d * float(CHUNK - 1))
        hop = jnp.exp(-d * float(CHUNK))
        state = jnp.zeros((1, width), jnp.float32)
        for k in range(chunks):
            rows = slice(k * CHUNK, (k + 1) * CHUNK)
            scaled = grow * g_ref[rows, :]
            high = scaled.astype(jnp.bfloat16)
            low = (scaled - high.astype(jnp.float32)).astype(jnp.bfloat16)
            y = jnp.dot(lower, high, preferred_element_type=jnp.float32) + jnp.dot(
                lower, low, preferred_element_type=jnp.float32
            )
            out_ref[rows, :] += shrink * y + after * state
            state = hop * state + tail * y[CHUNK - 1 : CHUNK, :]
        total_ref[pl.ds(r, 1), :] = state
        return carry

    for r in range(d_ref.shape[0]):
        mode(r, 0)


def packed_conv(packed, residues, decays, parts):
    seg, lanes = packed.shape
    width = lanes // parts
    modes = decays.shape[0]
    weight = residues * jnp.sqrt(-jnp.expm1(-2.0 * decays))
    decays_p = jnp.concatenate([decays] * parts, axis=1)
    weight_p = jnp.concatenate([weight] * parts, axis=1)
    local, ends = pl.pallas_call(
        conv_kernel,
        out_shape=(
            jax.ShapeDtypeStruct((seg, lanes), jnp.float32),
            jax.ShapeDtypeStruct(decays_p.shape, jnp.float32),
        ),
        interpret=INTERPRET,
    )(packed, decays_p, weight_p)
    ends = ends.reshape(modes, parts, width)
    index = jnp.arange(parts)
    lag = index[:, None] - 1 - index[None, :]
    gap = (float(seg) * jnp.maximum(lag, 0).astype(jnp.float32))[None, :, :, None]
    table = jnp.where((lag >= 0)[None, :, :, None], jnp.exp(-decays[:, None, None, :] * gap), 0.0)
    entry = jnp.sum(table * ends[:, None, :, :], axis=2).reshape(modes, lanes)
    steps = jnp.arange(seg, dtype=jnp.float32)
    after = jnp.exp(-decays_p[:, None, :] * (steps[None, :, None] + 1.0))
    return local + jnp.sum((weight_p * entry)[:, None, :] * after, axis=0)


def shards(
    query_input, key_input, value_input, short_filter, residues, decays, skip_gain, head_weight
):
    tokens, chan_width = query_input.shape
    width_v = lax.axis_size("v")
    piece = head_weight.shape[1]
    span = tokens * width_v
    parts = max(1, 128 // piece)
    seg = span // parts
    blocks = width_v // parts
    lanes = parts * piece
    def by_target(values):
        depth = values.shape[0]
        return jnp.transpose(values.reshape(depth, width_v, piece), (1, 0, 2))

    payload = jnp.concatenate(
        [by_target(key_input), by_target(value_input), by_target(query_input)], axis=1
    )
    depth = payload.shape[1]
    columns = lax.all_to_all(payload, "v", split_axis=0, concat_axis=0, tiled=True)
    columns = jnp.transpose(columns.reshape(parts, blocks, depth, piece), (1, 2, 0, 3))
    key_p, value_p, query_p = (
        columns[:, i * tokens : (i + 1) * tokens].reshape(seg, lanes) for i in range(3)
    )

    def behind(values):
        lead = jnp.zeros((2, piece), values.dtype)
        return jnp.concatenate([lead, values[-2:, : lanes - piece]], axis=1)

    head = lax.axis_index("v") * piece

    def own(values):
        return lax.dynamic_slice_in_dim(values, head, piece, axis=values.ndim - 1)

    sf = jnp.concatenate([own(short_filter)] * parts, axis=2)
    gain = jnp.concatenate([own(skip_gain)] * parts, axis=0)
    key_short = short_pass(key_p, behind(key_p), sf[:, 1])
    value_short = short_pass(value_p, behind(value_p), sf[:, 2])
    gated_p = (key_short * value_short).astype(jnp.bfloat16)
    query_short = short_pass(query_p, behind(query_p), sf[:, 0])
    convolved = packed_conv(gated_p, own(residues), own(decays), parts)
    carried = (convolved + gain * gated_p.astype(jnp.float32)).astype(jnp.bfloat16)
    op_p = (query_short * carried.astype(jnp.float32)).astype(jnp.bfloat16)
    following = jnp.concatenate(
        [op_p[:STRIDE, piece:], jnp.zeros((STRIDE, piece), op_p.dtype)], axis=1
    )
    extended = jnp.concatenate([op_p, following], axis=0)
    rows_seg = seg // STRIDE
    eye = jnp.eye(parts, dtype=head_weight.dtype)

    def spread(taps):
        return jnp.einsum("ico,ts->itcso", taps, eye).reshape(STRIDE * lanes, parts * taps.shape[2])

    early_rows = extended[:seg].reshape(rows_seg, STRIDE * lanes)
    late_rows = extended[STRIDE:].reshape(rows_seg, STRIDE * lanes)
    by_lane = jnp.dot(
        early_rows, spread(head_weight[:STRIDE]), preferred_element_type=jnp.float32
    ) + jnp.dot(late_rows, spread(head_weight[STRIDE:]), preferred_element_type=jnp.float32)
    per_block = tokens // STRIDE
    partial_sum = jnp.transpose(
        by_lane.reshape(blocks, per_block, parts, -1), (2, 0, 1, 3)
    ).reshape(width_v, per_block, -1)
    op_t = jnp.transpose(op_p.reshape(blocks, tokens, parts, piece), (2, 0, 1, 3))
    op_t = op_t.reshape(width_v, tokens, 1, 1, piece)
    sums = partial_sum.astype(jnp.bfloat16).reshape(width_v, -1, 1, 1, piece)
    outgoing = jnp.concatenate([op_t, sums], axis=1)
    incoming = lax.all_to_all(outgoing, "v", split_axis=0, concat_axis=3, tiled=True)[0]
    operator_out = incoming[:tokens].reshape(tokens, chan_width)
    sums = jnp.transpose(incoming[tokens:], (2, 0, 1, 3)).astype(jnp.float32)
    block_sum = jnp.sum(sums.reshape(width_v, tokens // STRIDE, -1), axis=0)
    probe_out = lax.psum_scatter(block_sum, "tp", scatter_dimension=0, tiled=True).astype(
        jnp.bfloat16
    )
    return (operator_out, probe_out)


def solution(mesh):
    seq_size, tp_size = mesh.devices.shape
    width_u = 1
    split = jax.sharding.Mesh(
        mesh.devices.reshape(width_u, seq_size // width_u, tp_size), ("u", "v", "tp")
    )
    seq = ("u", "v")
    placed = (
        P(seq, "tp"),
        P(seq, "tp"),
        P(seq, "tp"),
        P(None, None, "tp"),
        P(None, "tp"),
        P(None, "tp"),
        P("tp"),
        P(None, ("tp", "u", "v"), None),
    )
    return jax.shard_map(
        shards,
        mesh=split,
        in_specs=placed,
        out_specs=(P(seq, "tp"), P(("u", "v", "tp"), None)),
        check_vma=False,
    )
```

```python
import jax
import jax.numpy as jnp
from jax import lax
from jax.experimental import pallas as pl
from jax.sharding import PartitionSpec as P

STRIDE = 16
CHUNK = 128
INTERPRET = False

highest = lax.Precision.HIGHEST


def from_behind(block, axis, distance):
    devices = range(lax.axis_size(axis))
    route = [(i - distance, i) for i in devices if i - distance in devices]
    return lax.ppermute(block, axis, route)


def short_pass(rows, before, tap_weights):
    joined = jnp.concatenate([before, rows], axis=0).astype(jnp.float32)
    row_count = rows.shape[0]
    return (
        tap_weights[0] * joined[2 : 2 + row_count]
        + tap_weights[1] * joined[1 : 1 + row_count]
        + tap_weights[2] * joined[0:row_count]
    )


def conv_kernel(g_ref, d_ref, w_ref, out_ref, total_ref):
    span, width = g_ref.shape
    chunks = span // CHUNK
    row = lax.broadcasted_iota(jnp.int32, (CHUNK, CHUNK), 0)
    col = lax.broadcasted_iota(jnp.int32, (CHUNK, CHUNK), 1)
    lower = (row >= col).astype(jnp.bfloat16)
    steps = lax.broadcasted_iota(jnp.int32, (CHUNK, width), 0).astype(jnp.float32)

    def mode(r, carry):
        d = d_ref[pl.ds(r, 1), :]
        w = w_ref[pl.ds(r, 1), :]
        grow = jnp.exp(d * steps)
        shrink = w * jnp.exp(-d * steps)
        step = jnp.exp(-d)
        tail = jnp.exp(-d * float(CHUNK - 1))
        hop = jnp.exp(-d * float(CHUNK))
        state = jnp.zeros((1, width), jnp.float32)
        for k in range(chunks):
            rows = slice(k * CHUNK, (k + 1) * CHUNK)
            scaled = grow * g_ref[rows, :]
            high = scaled.astype(jnp.bfloat16)
            low = (scaled - high.astype(jnp.float32)).astype(jnp.bfloat16)
            y = jnp.dot(lower, high, preferred_element_type=jnp.float32) + jnp.dot(
                lower, low, preferred_element_type=jnp.float32
            )
            part = shrink * (y + step * state)
            if r == 0:
                out_ref[rows, :] = part
            else:
                out_ref[rows, :] += part
            state = hop * state + tail * y[CHUNK - 1 : CHUNK, :]
        total_ref[pl.ds(r, 1), :] = state
        return carry

    for r in range(d_ref.shape[0]):
        mode(r, 0)


def packed_conv(packed, residues, decays, parts):
    seg, lanes = packed.shape
    width = lanes // parts
    modes = decays.shape[0]
    weight = residues * jnp.sqrt(-jnp.expm1(-2.0 * decays))
    decays_p = jnp.concatenate([decays] * parts, axis=1)
    weight_p = jnp.concatenate([weight] * parts, axis=1)
    local, ends = pl.pallas_call(
        conv_kernel,
        out_shape=(
            jax.ShapeDtypeStruct((seg, lanes), jnp.float32),
            jax.ShapeDtypeStruct(decays_p.shape, jnp.float32),
        ),
        interpret=INTERPRET,
    )(packed, decays_p, weight_p)
    ends = ends.reshape(modes, parts, width)
    index = jnp.arange(parts)
    lag = index[:, None] - 1 - index[None, :]
    gap = (float(seg) * jnp.maximum(lag, 0).astype(jnp.float32))[None, :, :, None]
    table = jnp.where((lag >= 0)[None, :, :, None], jnp.exp(-decays[:, None, None, :] * gap), 0.0)
    entry = jnp.sum(table * ends[:, None, :, :], axis=2).reshape(modes, lanes)
    steps = jnp.arange(seg, dtype=jnp.float32)
    after = jnp.exp(-decays_p[:, None, :] * (steps[None, :, None] + 1.0))
    return local + jnp.sum((weight_p * entry)[:, None, :] * after, axis=0)


def shards(
    query_input, key_input, value_input, short_filter, residues, decays, skip_gain, head_weight
):
    tokens, chan_width = query_input.shape
    width_v = lax.axis_size("v")
    piece = head_weight.shape[1]
    span = tokens * width_v
    parts = max(1, 128 // piece)
    seg = span // parts
    blocks = width_v // parts
    lanes = parts * piece
    def by_target(values):
        depth = values.shape[0]
        return jnp.transpose(values.reshape(depth, width_v, piece), (1, 0, 2))

    payload = jnp.concatenate(
        [by_target(key_input), by_target(value_input), by_target(query_input)], axis=1
    )
    depth = payload.shape[1]
    columns = lax.all_to_all(payload, "v", split_axis=0, concat_axis=0, tiled=True)
    columns = jnp.transpose(columns.reshape(parts, blocks, depth, piece), (1, 2, 0, 3))
    key_p, value_p, query_p = (
        columns[:, i * tokens : (i + 1) * tokens].reshape(seg, lanes) for i in range(3)
    )

    def behind(values):
        lead = jnp.zeros((2, piece), values.dtype)
        return jnp.concatenate([lead, values[-2:, : lanes - piece]], axis=1)

    head = lax.axis_index("v") * piece

    def own(values):
        return lax.dynamic_slice_in_dim(values, head, piece, axis=values.ndim - 1)

    sf = jnp.concatenate([own(short_filter)] * parts, axis=2)
    gain = jnp.concatenate([own(skip_gain)] * parts, axis=0)
    key_short = short_pass(key_p, behind(key_p), sf[:, 1])
    value_short = short_pass(value_p, behind(value_p), sf[:, 2])
    gated_p = (key_short * value_short).astype(jnp.bfloat16)
    query_short = short_pass(query_p, behind(query_p), sf[:, 0])
    convolved = packed_conv(gated_p, own(residues), own(decays), parts)
    carried = (convolved + gain * gated_p.astype(jnp.float32)).astype(jnp.bfloat16)
    op_p = (query_short * carried.astype(jnp.float32)).astype(jnp.bfloat16)
    following = jnp.concatenate(
        [op_p[:STRIDE, piece:], jnp.zeros((STRIDE, piece), op_p.dtype)], axis=1
    )
    extended = jnp.concatenate([op_p, following], axis=0)
    rows_seg = seg // STRIDE
    eye = jnp.eye(parts, dtype=head_weight.dtype)

    def spread(taps):
        return jnp.einsum("ico,ts->itcso", taps, eye).reshape(STRIDE * lanes, parts * taps.shape[2])

    early_rows = extended[:seg].reshape(rows_seg, STRIDE * lanes)
    late_rows = extended[STRIDE:].reshape(rows_seg, STRIDE * lanes)
    by_lane = jnp.dot(
        early_rows, spread(head_weight[:STRIDE]), preferred_element_type=jnp.float32
    ) + jnp.dot(late_rows, spread(head_weight[STRIDE:]), preferred_element_type=jnp.float32)
    per_block = tokens // STRIDE
    partial_sum = jnp.transpose(
        by_lane.reshape(blocks, per_block, parts, -1), (2, 0, 1, 3)
    ).reshape(width_v, per_block, -1)
    op_t = jnp.transpose(op_p.reshape(blocks, tokens, parts, piece), (2, 0, 1, 3))
    op_t = op_t.reshape(width_v, tokens, 1, 1, piece)
    sums = partial_sum.astype(jnp.bfloat16).reshape(width_v, -1, 1, 1, piece)
    outgoing = jnp.concatenate([op_t, sums], axis=1)
    incoming = lax.all_to_all(outgoing, "v", split_axis=0, concat_axis=3, tiled=True)[0]
    operator_out = incoming[:tokens].reshape(tokens, chan_width)
    sums = jnp.transpose(incoming[tokens:], (2, 0, 1, 3)).astype(jnp.float32)
    block_sum = jnp.sum(sums.reshape(width_v, tokens // STRIDE, -1), axis=0)
    probe_out = lax.psum_scatter(block_sum, "tp", scatter_dimension=0, tiled=True).astype(
        jnp.bfloat16
    )
    return (operator_out, probe_out)


def solution(mesh):
    seq_size, tp_size = mesh.devices.shape
    width_u = 1
    split = jax.sharding.Mesh(
        mesh.devices.reshape(width_u, seq_size // width_u, tp_size), ("u", "v", "tp")
    )
    seq = ("u", "v")
    placed = (
        P(seq, "tp"),
        P(seq, "tp"),
        P(seq, "tp"),
        P(None, None, "tp"),
        P(None, "tp"),
        P(None, "tp"),
        P("tp"),
        P(None, ("tp", "u", "v"), None),
    )
    return jax.shard_map(
        shards,
        mesh=split,
        in_specs=placed,
        out_specs=(P(seq, "tp"), P(("u", "v", "tp"), None)),
        check_vma=False,
    )
```
